128 devices in a mesh: section: 4 (over x), dp: 32 (over y, z, core).
Axes of the slice: x: 4, y: 4, z: 4, core: 2. Of those that a mesh axis runs over, the one named last changes fastest.
Arguments:
- tokens: bfloat16 [4096, 8192], P('dp'), may hold values from -6 to 6
- cotangent: bfloat16 [4096, 8192], P('dp'), may hold values from -6 to 6
- gains: float32 [4, 8192], P('section'), may hold values from 0.5 to 1.5
- value_projection_weight: bfloat16 [4, 8192, 1024], P('section', 'dp'), may hold values from -0.0625 to 0.0625
- output_projection_weight: bfloat16 [4, 8192, 1024], P('section', 'dp'), may hold values from -0.1875 to 0.1875
- block_adapter_ids: int32 [32], replicated, may hold values from 0 to 63
- job_adapter: int32 [32, 64], replicated, may hold values from -1 to 63, as said below
- job_slab: int32 [32, 64], replicated, may hold values from -1 to 15, as said below
- token_counts: int32 [64], replicated, may hold values from 128 to 1023
- slot_adapter_params: bfloat16 [4, 2048, 9216], P('section', 'dp'), may hold values from -0.29882812 to 0.29882812
- first_moment: float32 [4, 2048, 9216], P('section', 'dp'), may hold values from -6 to 6
- second_moment: float32 [4, 2048, 9216], P('section', 'dp'), may hold values from 0.1 to 10
Outputs:
- new_params: bfloat16 [4, 2048, 9216], P('section', 'dp')
- new_first: float32 [4, 2048, 9216], P('section', 'dp')
- new_second: float32 [4, 2048, 9216], P('section', 'dp')
- user_panels: bfloat16 [4, 32, 147456], P('section', 'dp')
The draws below stay inside these ranges and needn't reach their ends.
Inputs may be any that keep to these rules, and one draw needn't show every extreme that they name: `job_adapter`: row o lists the adapters of which owner o holds a slab, each once, followed by -1; the 16 slabs of every adapter are held by 16 different owners, and every slab of every adapter is held exactly once. `job_slab`: the slab held in the same entry of job_adapter; -1 exactly where job_adapter is -1.
All inputs are finite; a program needn't handle non-finite values.
Results may differ from the reference program's by a relative error of at most 0.001.
Values may be sent and summed in bfloat16 or wider, within the bound.
No kernel may reach another device: no remote copies, remote signals or barrier semaphores. Data moves between devices by JAX's collectives and lax.ppermute only.
A program may use at most 128 MiB of HBM per device.

```python
import math
import jax
import jax.numpy as jnp
import numpy as np
from jax import lax

D = 8192
KVW = 1024
ADAPTER_RANK = 16
ADAPTERS = 64
BLOCK = 128
SECTIONS = 4
OWNERS = 32
NSLAB = 16
TOKENS = 4096
BLOCKS = 32
PARAMS = 147456
PANEL = 9216


def owner_plan(key):
    base_key = jax.random.fold_in(key, 11)
    key_center, key_offset = jax.random.split(base_key)
    center = jax.random.randint(key_center, (), 0, OWNERS)
    offsets = jax.random.randint(key_offset, (ADAPTERS,), 0, NSLAB)
    offsets = offsets.at[0].set(NSLAB - 1)
    starts = (center - offsets) % OWNERS
    owners = jnp.arange(OWNERS, dtype=jnp.int32)[:, None]
    slab_index = (owners - starts[None, :]) % OWNERS
    covered = slab_index < NSLAB
    list_rank = jnp.cumsum(covered.astype(jnp.int32), axis=1) - 1
    column = jnp.where(covered, list_rank, ADAPTERS)
    rows_grid = jnp.broadcast_to(owners, (OWNERS, ADAPTERS))
    adapter_grid = jnp.broadcast_to(jnp.arange(ADAPTERS, dtype=jnp.int32)[None, :], (OWNERS, ADAPTERS))
    empty_table = jnp.full((OWNERS, ADAPTERS), -1, jnp.int32)
    job_first = empty_table.at[rows_grid, column].set(adapter_grid, mode='drop')
    job_second = empty_table.at[rows_grid, column].set(slab_index.astype(jnp.int32), mode='drop')
    return (job_first, job_second)


def draw_job_adapter(key, part):
    return owner_plan(key)[0]


def draw_job_slab(key, part):
    return owner_plan(key)[1]


def plant(array, key, low, largest):
    spot = [jax.random.randint(jax.random.fold_in(key, axis), (), 0, length) for axis, length in enumerate(array.shape)]
    main_axis = array.shape.index(max(array.shape))
    beside = spot[:main_axis] + [(spot[main_axis] + 1) % array.shape[main_axis]] + spot[main_axis + 1:]
    return array.at[tuple(spot)].set(low).at[tuple(beside)].set(largest)


def block_levels(own_key, extent, cuts, low, largest):
    level = 1.0
    for axis_at, blocks in cuts:
        heights = jax.random.uniform(jax.random.fold_in(jax.random.fold_in(own_key, 6), axis_at), (blocks,), jnp.float32, low / len(cuts), largest / len(cuts))
        level = level * jnp.repeat(jnp.exp(heights), extent[axis_at] // blocks).reshape((-1,) + (1,) * (len(extent) - 1 - axis_at))
    return level


def rank_table(amount, lean):
    loads = [(1 << 20) // math.isqrt(rank ** lean) + 1 for rank in range(1, amount + 1)]
    scale = 1 + sum(loads) // (1 << 30)
    return np.cumsum(np.array([max(1, weight // scale) for weight in loads]))


def ranked(key, dims, amount, skew):
    grid = rank_table(amount, skew)
    lot = jax.random.randint(jax.random.fold_in(key, 1), dims, 0, int(grid[amount - 1]))
    rank = jnp.searchsorted(jnp.asarray(grid, jnp.int32), lot, side="right")
    return jax.random.permutation(jax.random.fold_in(key, 2), amount)[rank].astype(jnp.int32)


def scatter_about(own_key, extent, width, most, shards=(), kind=jnp.bfloat16):
    entries = jax.random.normal(own_key, extent, jnp.float32) * width
    if len(shards) > 0:
        entries = block_levels(own_key, extent, shards, -0.22, 0.18) * entries
    return jnp.clip(entries, min=-most, max=most).astype(kind)


def setup_inputs(seed: int = 0) -> dict:
    streams_of = jax.random.split(jax.random.key(seed), 13)
    tokens = scatter_about(streams_of[0], (TOKENS, D), 1.0, 6.0, ((0, 32),))
    cotangent = scatter_about(streams_of[1], (TOKENS, D), 1.0, 6.0, ((0, 32),))
    gains = jnp.clip(1.0 + 0.1 * jax.random.normal(streams_of[2], (SECTIONS, D), jnp.float32), 0.5, 1.5)
    value_projection_weight = scatter_about(streams_of[3], (SECTIONS, D, KVW), D ** -0.5, 0.0625, ((0, 4), (1, 32)))
    output_projection_weight = scatter_about(streams_of[4], (SECTIONS, D, KVW), KVW ** -0.5, 0.1875, ((0, 4), (1, 32)))
    block_adapter_ids = plant(ranked(streams_of[5], (BLOCKS,), ADAPTERS, 2), jax.random.fold_in(streams_of[5], 3), 0, ADAPTERS - 1).astype(jnp.int32)
    job_adapter = draw_job_adapter(jax.random.fold_in(streams_of[12], 71), 0)
    job_slab = draw_job_slab(jax.random.fold_in(streams_of[12], 71), 0)
    token_counts = plant(jax.random.randint(streams_of[8], (ADAPTERS,), BLOCK, 8 * BLOCK), jax.random.fold_in(streams_of[8], 1), BLOCK, (8 * BLOCK) - 1).astype(jnp.int32)
    slot_adapter_params = scatter_about(streams_of[9], (SECTIONS, OWNERS * ADAPTERS, PANEL), 0.05, 0.29882812, ((0, 4), (1, 32)))
    first_moment = scatter_about(streams_of[10], (SECTIONS, OWNERS * ADAPTERS, PANEL), 1.0, 6.0, ((0, 4), (1, 32)), jnp.float32)
    second_moment = jnp.clip(jnp.exp(math.log(10.0) - 4.6051702 * jax.random.uniform(streams_of[11], (SECTIONS, OWNERS * ADAPTERS, PANEL), jnp.float32) ** block_levels(streams_of[11], (SECTIONS, OWNERS * ADAPTERS, PANEL), ((0, 4), (1, 32)), -0.2, 0.2)), 0.1, 10.0)
    return {"tokens": tokens, "cotangent": cotangent, "gains": gains, "value_projection_weight": value_projection_weight, "output_projection_weight": output_projection_weight, "block_adapter_ids": block_adapter_ids, "job_adapter": job_adapter, "job_slab": job_slab, "token_counts": token_counts, "slot_adapter_params": slot_adapter_params, "first_moment": first_moment, "second_moment": second_moment}


ADAPTER_SCALE = 2.0
LEARN_RATE = 0.001
BETA_FIRST = 0.9
BETA_SECOND = 0.999
ADAM_EPS = 1e-08
FIRST_FIX = 1.0 - 0.9 ** 50 * 0.9 ** 50
SECOND_FIX = 1.0 - 0.999 ** 50 * 0.999 ** 50
NORM_EPS = 1e-05

def contract_trailing(left, right):
    return lax.dot_general(left, right, (((1,), (1,)), ((), ())), preferred_element_type=jnp.float32)

def contract_leading(left, right):
    return lax.dot_general(left, right, (((0,), (0,)), ((), ())), preferred_element_type=jnp.float32)

def norm_rows(hidden_state, gain_vector_row):
    hidden_wide = hidden_state.astype(jnp.float32)
    mean_square = lax.optimization_barrier(jnp.mean(hidden_wide * hidden_wide, axis=-1, keepdims=True))
    norm_gain_scale = lax.rsqrt(mean_square + NORM_EPS)
    normalized_rows = (hidden_wide * norm_gain_scale * gain_vector_row).astype(jnp.bfloat16)
    return (hidden_wide, norm_gain_scale, normalized_rows)

def layer_ahead_pass(hidden_state, gain_vector_row, value_complete, output_complete, adapter_down, adapter_up):
    hidden_wide, norm_gain_scale, normalized_rows = norm_rows(hidden_state, gain_vector_row)
    rank_projected = jnp.dot(normalized_rows, adapter_down, preferred_element_type=jnp.float32).astype(jnp.bfloat16)
    value_block_rows = (jnp.dot(normalized_rows, value_complete, preferred_element_type=jnp.float32) + ADAPTER_SCALE * jnp.dot(rank_projected, adapter_up, preferred_element_type=jnp.float32)).astype(jnp.bfloat16)
    output_block_rows = (hidden_wide + contract_trailing(value_block_rows, output_complete)).astype(jnp.bfloat16)
    return (output_block_rows, norm_gain_scale, normalized_rows, rank_projected)

def layer_reverse_pass(output_gradient, hidden_state, norm_gain_scale, normalized_rows, rank_projected, gain_vector_row, value_complete, output_complete, adapter_down, adapter_up):
    value_gradient = jnp.dot(output_gradient, output_complete, preferred_element_type=jnp.float32).astype(jnp.bfloat16)
    low_rank_gradient = (ADAPTER_SCALE * contract_trailing(value_gradient, adapter_up)).astype(jnp.bfloat16)
    down_gradient = contract_leading(normalized_rows, low_rank_gradient)
    up_gradient = ADAPTER_SCALE * contract_leading(rank_projected, value_gradient)
    normed_gradient = (contract_trailing(value_gradient, value_complete) + contract_trailing(low_rank_gradient, adapter_down)) * gain_vector_row
    hidden_wide = hidden_state.astype(jnp.float32)
    centred = lax.optimization_barrier(jnp.mean(hidden_wide * normed_gradient, axis=-1, keepdims=True))
    grad_in = output_gradient.astype(jnp.float32) + norm_gain_scale * normed_gradient - hidden_wide * norm_gain_scale ** 3 * centred
    return (grad_in.astype(jnp.bfloat16), down_gradient, up_gradient)

def adam_update(params_old, first_old, second_old, slot_grad, live):
    first_step = BETA_FIRST * first_old + (1.0 - BETA_FIRST) * slot_grad
    second_step = BETA_SECOND * second_old + (1.0 - BETA_SECOND) * slot_grad * slot_grad
    step_size = first_step / FIRST_FIX / (jnp.sqrt(second_step / SECOND_FIX) + ADAM_EPS)
    params_step = (params_old.astype(jnp.float32) - LEARN_RATE * step_size).astype(jnp.bfloat16)
    return (jnp.where(live, params_step, params_old), jnp.where(live, first_step, first_old), jnp.where(live, second_step, second_old))

def reference(tokens, cotangent, gains, value_projection_weight, output_projection_weight, block_adapter_ids, job_adapter, job_slab, token_counts, slot_adapter_params, first_moment, second_moment):
    flat_jobs = job_adapter.reshape(-1)
    flat_slabs = job_slab.reshape(-1)
    live = flat_jobs >= 0
    target = jnp.where(live, flat_jobs, ADAPTERS).astype(jnp.int32)
    slab_safe = jnp.where(live, flat_slabs, 0).astype(jnp.int32)
    divide_position = D * ADAPTER_RANK

    def build_lookup_table(owned):
        table = jnp.zeros((ADAPTERS + 1, NSLAB, PANEL), owned.dtype).at[target, slab_safe].set(owned)
        return table[:ADAPTERS].reshape(ADAPTERS, PARAMS)

    def divide_parameters(vectors):
        return (vectors[:, :divide_position].reshape(-1, D, ADAPTER_RANK), vectors[:, divide_position:].reshape(-1, ADAPTER_RANK, KVW))
    ahead_block_map = jax.vmap(layer_ahead_pass, in_axes=(0, None, None, None, 0, 0))
    reverse_block_map = jax.vmap(layer_reverse_pass, in_axes=(0, 0, 0, 0, 0, None, None, None, 0, 0))
    hidden_state = tokens.reshape(BLOCKS, BLOCK, D)
    residuals_kept = []
    for section_count_total in range(SECTIONS):
        adapter_down, adapter_up = divide_parameters(build_lookup_table(slot_adapter_params[section_count_total])[block_adapter_ids])
        output_block_rows, norm_gain_scale, normalized_rows, rank_projected = ahead_block_map(hidden_state, gains[section_count_total], value_projection_weight[section_count_total], output_projection_weight[section_count_total], adapter_down, adapter_up)
        residuals_kept.append((hidden_state, norm_gain_scale, normalized_rows, rank_projected, adapter_down, adapter_up))
        hidden_state = output_block_rows
    row_gradients = cotangent.reshape(BLOCKS, BLOCK, D)
    params_list, first_list, second_list, user_list = ([], [], [], [])
    counts_padded = jnp.concatenate([token_counts, jnp.ones((1,), jnp.int32)]).astype(jnp.float32)
    for section_count_total in reversed(range(SECTIONS)):
        hidden_input, norm_gain_scale, normalized_rows, rank_projected, adapter_down, adapter_up = residuals_kept[section_count_total]
        row_gradients, down_gradient, up_gradient = reverse_block_map(row_gradients, hidden_input, norm_gain_scale, normalized_rows, rank_projected, gains[section_count_total], value_projection_weight[section_count_total], output_projection_weight[section_count_total], adapter_down, adapter_up)
        block_grads = jnp.concatenate([down_gradient.reshape(BLOCKS, -1), up_gradient.reshape(BLOCKS, -1)], axis=1)
        adapter_grads = jax.ops.segment_sum(block_grads, block_adapter_ids, num_segments=ADAPTERS)
        adapter_grads = jnp.concatenate([adapter_grads.reshape(ADAPTERS, NSLAB, PANEL), jnp.zeros((1, NSLAB, PANEL), jnp.float32)], axis=0)
        slot_grad = adapter_grads[target, slab_safe] / counts_padded[target][:, None]
        params_new, first_new, second_new = adam_update(slot_adapter_params[section_count_total], first_moment[section_count_total], second_moment[section_count_total], slot_grad, live[:, None])
        params_list.append(params_new)
        first_list.append(first_new)
        second_list.append(second_new)
        user_list.append(build_lookup_table(params_new)[block_adapter_ids])
    order = list(reversed(range(SECTIONS)))
    return (jnp.stack([params_list[i] for i in order]), jnp.stack([first_list[i] for i in order]), jnp.stack([second_list[i] for i in order]), jnp.stack([user_list[i] for i in order]))
```

```python
import jax
import jax.numpy as jnp
from jax import lax
from jax.experimental import pallas as pl
from jax.experimental.pallas import tpu as pltpu
from jax.sharding import PartitionSpec as P

ADAPTER_RANK = 16
MICRO = 4
LAG = 2
CHUNK = 1024

ADAPTER_SCALE = 2.0
LEARN_RATE = 0.001
BETA_FIRST = 0.9
BETA_SECOND = 0.999
ADAM_EPS = 1e-08
FIRST_FIX = 1.0 - 0.9**50 * 0.9**50
SECOND_FIX = 1.0 - 0.999**50 * 0.999**50
NORM_EPS = 1e-05
F32 = jnp.float32
BF16 = jnp.bfloat16


def contract_trailing(left, right):
    return lax.dot_general(
        left, right, (((1,), (1,)), ((), ())), preferred_element_type=F32
    )


def contract_leading(left, right):
    return lax.dot_general(
        left, right, (((0,), (0,)), ((), ())), preferred_element_type=F32
    )


def plain_dot(left, right):
    return jnp.dot(left, right, preferred_element_type=F32)


def ahead_kernel(h_ref, down_ref, up_ref, value_ref, output_ref, next_ref, u_ref, low_ref, scale_ref, sum_ref, v_ref):
    step = pl.program_id(0)
    chunks = pl.num_programs(0) // 2
    width = h_ref.shape[1] * chunks

    @pl.when(step == 0)
    def _():
        u_ref[...] = jnp.zeros_like(u_ref)
        low_ref[...] = jnp.zeros_like(low_ref)
        sum_ref[...] = jnp.zeros_like(sum_ref)

    @pl.when(step < chunks)
    def _():
        rows = h_ref[...]
        wide = rows.astype(F32)
        u_ref[...] += plain_dot(rows, value_ref[...])
        low_ref[...] += contract_trailing(rows, down_ref[...])
        sum_ref[...] += jnp.sum(wide * wide, axis=-1, keepdims=True)

    @pl.when(step == chunks - 1)
    def _():
        scale = lax.rsqrt(sum_ref[...] / width + NORM_EPS)
        scale_ref[...] = scale
        low = (scale * low_ref[...]).astype(BF16)
        v_ref[...] = (
            scale * u_ref[...] + ADAPTER_SCALE * plain_dot(low, up_ref[...])
        ).astype(BF16)

    @pl.when(step >= chunks)
    def _():
        next_ref[...] = (
            h_ref[...].astype(F32) + contract_trailing(v_ref[...], output_ref[...])
        ).astype(BF16)


def ahead(hidden, down_t, up, value_full, output_full):
    rows, width = hidden.shape
    features = up.shape[1]
    chunks = width // CHUNK
    whole = lambda i: (0, 0)
    return pl.pallas_call(
        ahead_kernel,
        grid=(2 * chunks,),
        in_specs=[
            pl.BlockSpec((rows, CHUNK), lambda i: (0, i % chunks)),
            pl.BlockSpec((ADAPTER_RANK, CHUNK), lambda i: (0, jnp.minimum(i, chunks - 1))),
            pl.BlockSpec((ADAPTER_RANK, features), whole),
            pl.BlockSpec((CHUNK, features), lambda i: (jnp.minimum(i, chunks - 1), 0)),
            pl.BlockSpec((CHUNK, features), lambda i: (jnp.maximum(i - chunks, 0), 0)),
        ],
        out_specs=(
            pl.BlockSpec((rows, CHUNK), lambda i: (0, jnp.maximum(i - chunks, 0))),
            pl.BlockSpec((rows, features), whole),
            pl.BlockSpec((rows, ADAPTER_RANK), whole),
            pl.BlockSpec((rows, 1), whole),
        ),
        out_shape=(
            jax.ShapeDtypeStruct((rows, width), BF16),
            jax.ShapeDtypeStruct((rows, features), F32),
            jax.ShapeDtypeStruct((rows, ADAPTER_RANK), F32),
            jax.ShapeDtypeStruct((rows, 1), F32),
        ),
        scratch_shapes=[
            pltpu.VMEM((rows, 1), F32),
            pltpu.VMEM((rows, features), BF16),
        ],
        compiler_params=pltpu.CompilerParams(vmem_limit_bytes=24 * 2**20),
        name="ahead",
    )(hidden, down_t, up, value_full, output_full)


def reverse_kernel(
    grad_ref, output_ref, value_ref, down_ref, up_ref, h_ref, u_ref, low_ref, scale_ref,
    prev_ref, gv_ref, gl_ref, acc_ref, coef_ref,
):
    step = pl.program_id(0)
    chunks = pl.num_programs(0) // 2
    width = grad_ref.shape[1] * chunks

    @pl.when(step == 0)
    def _():
        acc_ref[...] = jnp.zeros_like(acc_ref)

    @pl.when(step < chunks)
    def _():
        acc_ref[...] += plain_dot(grad_ref[...], output_ref[...])

    @pl.when(step == chunks - 1)
    def _():
        gv = acc_ref[...].astype(BF16)
        gl = (ADAPTER_SCALE * contract_trailing(gv, up_ref[...])).astype(BF16)
        gv_ref[...] = gv
        gl_ref[...] = gl
        scale = scale_ref[...]
        centred = (
            jnp.sum(gv.astype(F32) * u_ref[...], axis=-1, keepdims=True)
            + jnp.sum(gl.astype(F32) * low_ref[...], axis=-1, keepdims=True)
        ) / width
        coef_ref[...] = scale * scale * scale * centred

    @pl.when(step >= chunks)
    def _():
        grad_norm = contract_trailing(gv_ref[...], value_ref[...]) + plain_dot(gl_ref[...], down_ref[...])
        prev_ref[...] = (
            grad_ref[...].astype(F32)
            + scale_ref[...] * grad_norm
            - h_ref[...].astype(F32) * coef_ref[...]
        ).astype(BF16)


def reverse(grad, output_full, value_full, down_t, up, hidden, u, low, scale):
    rows, width = grad.shape
    features = up.shape[1]
    chunks = width // CHUNK
    whole = lambda i: (0, 0)
    late = lambda i: (0, jnp.maximum(i - chunks, 0))
    return pl.pallas_call(
        reverse_kernel,
        grid=(2 * chunks,),
        in_specs=[
            pl.BlockSpec((rows, CHUNK), lambda i: (0, i % chunks)),
            pl.BlockSpec((CHUNK, features), lambda i: (jnp.minimum(i, chunks - 1), 0)),
            pl.BlockSpec((CHUNK, features), lambda i: (jnp.maximum(i - chunks, 0), 0)),
            pl.BlockSpec((ADAPTER_RANK, CHUNK), late),
            pl.BlockSpec((ADAPTER_RANK, features), whole),
            pl.BlockSpec((rows, CHUNK), late),
            pl.BlockSpec((rows, features), whole),
            pl.BlockSpec((rows, ADAPTER_RANK), whole),
            pl.BlockSpec((rows, 1), whole),
        ],
        out_specs=(
            pl.BlockSpec((rows, CHUNK), late),
            pl.BlockSpec((rows, features), whole),
            pl.BlockSpec((rows, ADAPTER_RANK), whole),
        ),
        out_shape=(
            jax.ShapeDtypeStruct((rows, width), BF16),
            jax.ShapeDtypeStruct((rows, features), BF16),
            jax.ShapeDtypeStruct((rows, ADAPTER_RANK), BF16),
        ),
        scratch_shapes=[pltpu.VMEM((rows, features), F32), pltpu.VMEM((rows, 1), F32)],
        compiler_params=pltpu.CompilerParams(vmem_limit_bytes=24 * 2**20),
        name="reverse",
    )(grad, output_full, value_full, down_t, up, hidden, u, low, scale)


def first_kernel(grad_ref, output_ref, up_ref, gv_ref, gl_ref, acc_ref):
    step = pl.program_id(0)

    @pl.when(step == 0)
    def _():
        acc_ref[...] = jnp.zeros_like(acc_ref)

    acc_ref[...] += plain_dot(grad_ref[...], output_ref[...])

    @pl.when(step == pl.num_programs(0) - 1)
    def _():
        gv = acc_ref[...].astype(BF16)
        gv_ref[...] = gv
        gl_ref[...] = (ADAPTER_SCALE * contract_trailing(gv, up_ref[...])).astype(BF16)


def reverse_first(grad, output_full, up):
    rows, width = grad.shape
    features = up.shape[1]
    whole = lambda i: (0, 0)
    return pl.pallas_call(
        first_kernel,
        grid=(width // CHUNK,),
        in_specs=[
            pl.BlockSpec((rows, CHUNK), lambda i: (0, i)),
            pl.BlockSpec((CHUNK, features), lambda i: (i, 0)),
            pl.BlockSpec((ADAPTER_RANK, features), whole),
        ],
        out_specs=(pl.BlockSpec((rows, features), whole), pl.BlockSpec((rows, ADAPTER_RANK), whole)),
        out_shape=(
            jax.ShapeDtypeStruct((rows, features), BF16),
            jax.ShapeDtypeStruct((rows, ADAPTER_RANK), BF16),
        ),
        scratch_shapes=[pltpu.VMEM((rows, features), F32)],
        compiler_params=pltpu.CompilerParams(vmem_limit_bytes=16 * 2**20),
        name="reverse_first",
    )(grad, output_full, up)


def spread_kernel(gv_ref, gl_ref, value_ref, down_ref, out_ref):
    out_ref[...] = contract_trailing(gv_ref[...], value_ref[...]) + plain_dot(gl_ref[...], down_ref[...])


def spread(gv, gl, value_full, down_t):
    rows, features = gv.shape
    width = value_full.shape[0]
    whole = lambda i: (0, 0)
    return pl.pallas_call(
        spread_kernel,
        grid=(width // CHUNK,),
        in_specs=[
            pl.BlockSpec((rows, features), whole),
            pl.BlockSpec((rows, ADAPTER_RANK), whole),
            pl.BlockSpec((CHUNK, features), lambda i: (i, 0)),
            pl.BlockSpec((ADAPTER_RANK, CHUNK), lambda i: (0, i)),
        ],
        out_specs=pl.BlockSpec((rows, CHUNK), lambda i: (0, i)),
        out_shape=jax.ShapeDtypeStruct((rows, width), F32),
        compiler_params=pltpu.CompilerParams(vmem_limit_bytes=16 * 2**20),
        name="spread",
    )(gv, gl, value_full, down_t)


def join_kernel(h_ref, norm_ref, grad_ref, down_ref, prev_ref, low_ref, scale_ref):
    width = h_ref.shape[1]
    rows = h_ref[...]
    wide = rows.astype(F32)
    grad_norm = norm_ref[...]
    low_ref[...] = contract_trailing(rows, down_ref[...])
    scale = lax.rsqrt(jnp.sum(wide * wide, axis=-1, keepdims=True) / width + NORM_EPS)
    scale_ref[...] = scale
    centred = jnp.sum(wide * grad_norm, axis=-1, keepdims=True) / width
    prev_ref[...] = (
        grad_ref[...].astype(F32) + scale * grad_norm - wide * (scale * scale * scale * centred)
    ).astype(BF16)


def join_last(hidden, grad_norm, grad, down_t):
    rows, width = hidden.shape
    return pl.pallas_call(
        join_kernel,
        out_shape=(
            jax.ShapeDtypeStruct((rows, width), BF16),
            jax.ShapeDtypeStruct((rows, ADAPTER_RANK), F32),
            jax.ShapeDtypeStruct((rows, 1), F32),
        ),
        compiler_params=pltpu.CompilerParams(vmem_limit_bytes=24 * 2**20),
        name="join_last",
    )(hidden, grad_norm, grad, down_t)


def adam_update(params_old, first_old, second_old, slot_grad, live):
    first_step = BETA_FIRST * first_old + (1.0 - BETA_FIRST) * slot_grad
    second_step = BETA_SECOND * second_old + (1.0 - BETA_SECOND) * slot_grad * slot_grad
    step_size = first_step / FIRST_FIX / (jnp.sqrt(second_step / SECOND_FIX) + ADAM_EPS)
    params_step = (params_old.astype(jnp.float32) - LEARN_RATE * step_size).astype(jnp.bfloat16)
    return (
        jnp.where(live, params_step, params_old),
        jnp.where(live, first_step, first_old),
        jnp.where(live, second_step, second_old),
    )


def on_device(
    tokens,
    cotangent,
    gains,
    value_projection_weight,
    output_projection_weight,
    block_adapter_ids,
    job_adapter,
    job_slab,
    token_counts,
    slot_adapter_params,
    first_moment,
    second_moment,
):
    section_index = lax.axis_index("section")
    owner_index = lax.axis_index("dp")
    section_total = lax.axis_size("section")
    owner_total = lax.axis_size("dp")
    tok_dev, hidden_width = tokens.shape
    value_feature_width = value_projection_weight.shape[2]
    panel_width = slot_adapter_params.shape[2]
    slab_count = owner_total // 2
    block_total = block_adapter_ids.shape[0]
    local_blocks = block_total // owner_total
    block_rows = tok_dev // local_blocks
    adapter_total = token_counts.shape[0]
    divide_position = hidden_width * ADAPTER_RANK
    gain_row = gains[0]
    shard_rows = value_projection_weight.shape[1]
    my_gain = lax.dynamic_slice_in_dim(gain_row, owner_index * shard_rows, shard_rows)
    scaled_value = (value_projection_weight[0].astype(F32) * my_gain[:, None]).astype(BF16)
    value_full = lax.all_gather(scaled_value, "dp", axis=0, tiled=True)
    output_full = lax.all_gather(output_projection_weight[0], "dp", axis=0, tiled=True)
    my_jobs = lax.dynamic_index_in_dim(job_adapter, owner_index, 0, keepdims=False)
    my_blocks = lax.dynamic_slice_in_dim(
        block_adapter_ids, owner_index * local_blocks, local_blocks
    )
    slab_ids = jnp.arange(slab_count, dtype=jnp.int32)
    matching = (job_adapter[None, None] == my_blocks[:, None, None, None]) & (
        job_slab[None, None] == slab_ids[None, :, None, None]
    )
    owner_ids = jnp.arange(owner_total, dtype=jnp.int32)
    source_owner = jnp.sum(jnp.where(matching, owner_ids[None, None, :, None], 0), axis=(2, 3))
    own_select = (block_adapter_ids[:, None] == my_jobs[None, :]) & (my_jobs[None, :] >= 0)
    slot_rows = jnp.arange(local_blocks, dtype=jnp.int32)[:, None]

    def hand_out(owned):
        picked = jnp.dot(own_select.astype(jnp.bfloat16), owned, preferred_element_type=jnp.float32)
        return picked.astype(jnp.bfloat16).reshape(owner_total, local_blocks, panel_width)

    def assemble(arrived):
        gathered_slabs = arrived[source_owner, slot_rows]
        return gathered_slabs.reshape(local_blocks, slab_count * panel_width)

    gathered_panels = assemble(
        lax.all_to_all(
            hand_out(slot_adapter_params[0]), "dp", split_axis=0, concat_axis=0, tiled=True
        )
    )
    down_t = (
        gathered_panels[0, :divide_position].reshape(hidden_width, ADAPTER_RANK).T.astype(F32)
        * gain_row[None, :]
    ).astype(BF16)
    up = gathered_panels[0, divide_position:].reshape(ADAPTER_RANK, value_feature_width)
    rows = tok_dev // MICRO
    last = section_total - 1
    token_micro = [tokens[m * rows : (m + 1) * rows] for m in range(MICRO)]
    cot_micro = [cotangent[m * rows : (m + 1) * rows] for m in range(MICRO)]
    ahead_pairs = [(i, i + 1) for i in range(last)]
    back_pairs = [(i + 1, i) for i in range(last)]
    wide_zero = lambda: jnp.zeros((rows, hidden_width), BF16)

    def prepare_last(_):
        gv, gl = reverse_first(cotangent, output_full, up)
        return gv, gl, spread(gv, gl, value_full, down_t)

    def prepare_none(_):
        return (
            jnp.zeros((tok_dev, value_feature_width), BF16),
            jnp.zeros((tok_dev, ADAPTER_RANK), BF16),
            jnp.zeros((tok_dev, hidden_width), F32),
        )

    last_gv, last_gl, last_norm = lax.cond(section_index == last, prepare_last, prepare_none, None)

    entering, ahead_state, ahead_sent = {}, {}, {}
    back_state, back_sent, last_state = {}, {}, {}
    for step in range(2 * last * LAG + MICRO):
        active = [s for s in range(last) if 0 <= step - LAG * s < MICRO]
        if step - LAG in ahead_sent:
            entering[step] = ahead_sent[step - LAG]
        if active:
            if step < MICRO:
                entering[step] = (
                    jnp.where(section_index == 0, token_micro[step], entering[step])
                    if step in entering
                    else token_micro[step]
                )
            is_active = (section_index >= active[0]) & (section_index <= active[-1])
            shape_of = jax.eval_shape(ahead, entering[step], down_t, up, value_full, output_full)
            result = lax.cond(
                is_active,
                lambda h: tuple(ahead(h, down_t, up, value_full, output_full)),
                lambda h: tuple(jnp.zeros(x.shape, x.dtype) for x in shape_of),
                entering[step],
            )
            ahead_state[step] = result[1:]
            ahead_sent[step] = lax.ppermute(result[0], "section", ahead_pairs)
        m_last = step - LAG * last
        branch = {}
        if 0 <= m_last < MICRO:
            branch[last] = m_last
        for s in range(last):
            m = step - LAG * (2 * last - s)
            if 0 <= m < MICRO:
                branch[s] = m
        if branch:
            incoming = back_sent.get(step - LAG)

            def nothing(_):
                return (
                    wide_zero(),
                    jnp.zeros((rows, value_feature_width), BF16),
                    jnp.zeros((rows, ADAPTER_RANK), BF16),
                    jnp.zeros((rows, ADAPTER_RANK), F32),
                    jnp.zeros((rows, 1), F32),
                )

            def make(s, m):
                def run_last(_):
                    prev, low, scale = join_last(
                        entering[step],
                        last_norm[m * rows : (m + 1) * rows],
                        cot_micro[m],
                        down_t,
                    )
                    return (prev,) + nothing(None)[1:3] + (low, scale)

                def run_first(_):
                    gv, gl = reverse_first(incoming, output_full, up)
                    return (wide_zero(), gv, gl) + nothing(None)[3:]

                def run_middle(_):
                    before = LAG * s + m
                    u, low, scale = ahead_state[before]
                    prev, gv, gl = reverse(
                        incoming, output_full, value_full, down_t, up, entering[before], u, low, scale
                    )
                    return (prev, gv, gl) + nothing(None)[3:]

                return run_last if s == last else run_first if s == 0 else run_middle

            result = lax.switch(
                section_index,
                [make(s, branch[s]) if s in branch else nothing for s in range(section_total)],
                None,
            )
            back_state[step] = result[1:3]
            last_state[step] = result[3:]
            if any(s > 0 for s in branch):
                back_sent[step] = lax.ppermute(result[0], "section", back_pairs)

    def gradients(s):
        def run(_):
            if s == last:
                steps = [LAG * last + m for m in range(MICRO)]
                gv, gl = last_gv, last_gl
                low = jnp.concatenate([last_state[k][0] for k in steps])
                scale = jnp.concatenate([last_state[k][1] for k in steps])
            else:
                steps = [LAG * s + m for m in range(MICRO)]
                later = [LAG * (2 * last - s) + m for m in range(MICRO)]
                gv = jnp.concatenate([back_state[k][0] for k in later])
                gl = jnp.concatenate([back_state[k][1] for k in later])
                low = jnp.concatenate([ahead_state[k][1] for k in steps])
                scale = jnp.concatenate([ahead_state[k][2] for k in steps])
            hidden = jnp.concatenate([entering[k] for k in steps]) if s else tokens
            scaled = (scale * gl.astype(F32)).astype(BF16)
            down_grad = contract_leading(hidden, scaled) * gain_row[:, None]
            low_rows = (scale * low).astype(BF16)
            up_grad = ADAPTER_SCALE * contract_leading(low_rows, gv)
            return jnp.concatenate(
                [down_grad.astype(BF16).reshape(-1), up_grad.astype(BF16).reshape(-1)]
            )

        return run

    block_grads = lax.switch(section_index, [gradients(s) for s in range(section_total)], None)
    outgoing = (
        jnp.zeros((owner_total, local_blocks, panel_width), BF16)
        .at[source_owner, slot_rows]
        .set(block_grads.reshape(local_blocks, slab_count, panel_width))
    )
    arrived = lax.all_to_all(outgoing, "dp", split_axis=0, concat_axis=0, tiled=True)
    summed = jnp.dot(
        own_select.astype(BF16).T,
        arrived.reshape(block_total, panel_width),
        preferred_element_type=F32,
    )
    live = my_jobs >= 0
    adapter_ids = jnp.arange(adapter_total, dtype=jnp.int32)
    slot_counts = jnp.sum(
        jnp.where(adapter_ids[None, :] == my_jobs[:, None], token_counts[None, :], 0), axis=1
    )
    slot_counts = jnp.where(live, slot_counts, 1)
    slot_grad = summed / slot_counts.astype(jnp.float32)[:, None]
    params_new, first_new, second_new = adam_update(
        slot_adapter_params[0], first_moment[0], second_moment[0], slot_grad, live[:, None]
    )
    returned = assemble(
        lax.all_to_all(hand_out(params_new), "dp", split_axis=0, concat_axis=0, tiled=True)
    )
    return (params_new[None], first_new[None], second_new[None], returned[None])


def solution(mesh):
    return jax.shard_map(
        on_device,
        mesh=mesh,
        in_specs=(
            P("dp", None),
            P("dp", None),
            P("section", None),
            P("section", "dp", None),
            P("section", "dp", None),
            P(),
            P(),
            P(),
            P(),
            P("section", "dp", None),
            P("section", "dp", None),
            P("section", "dp", None),
        ),
        out_specs=(
            P("section", "dp", None),
            P("section", "dp", None),
            P("section", "dp", None),
            P("section", "dp", None),
        ),
        check_vma=False,
    )
```

```python
import jax
import jax.numpy as jnp
from jax import lax
from jax.experimental import pallas as pl
from jax.experimental.pallas import tpu as pltpu
from jax.sharding import PartitionSpec as P

ADAPTER_RANK = 16
MICRO = 4
LIMIT = 4
SECTIONS = 4
LAG = 2
CHUNK = 1024
RING = 4

ADAPTER_SCALE = 2.0
LEARN_RATE = 0.001
BETA_FIRST = 0.9
BETA_SECOND = 0.999
ADAM_EPS = 1e-08
FIRST_FIX = 1.0 - 0.9**50 * 0.9**50
SECOND_FIX = 1.0 - 0.999**50 * 0.999**50
NORM_EPS = 1e-05
F32 = jnp.float32
BF16 = jnp.bfloat16


def contract_trailing(left, right):
    return lax.dot_general(
        left, right, (((1,), (1,)), ((), ())), preferred_element_type=F32
    )


def contract_leading(left, right):
    return lax.dot_general(
        left, right, (((0,), (0,)), ((), ())), preferred_element_type=F32
    )


def plain_dot(left, right):
    return jnp.dot(left, right, preferred_element_type=F32)


def window(i):
    return pl.ds(pl.multiple_of(i * CHUNK, CHUNK), CHUNK)


VMEM_SPEC = pl.BlockSpec(memory_space=pltpu.VMEM)
SMEM_SPEC = pl.BlockSpec(memory_space=pltpu.SMEM)
FAR_SPEC = pl.BlockSpec(memory_space=pltpu.HBM)


def load_weight(pieces, lanes, section):
    features = lanes.stop - lanes.start
    width = sum(piece.shape[0] for piece in pieces)

    def kernel(*refs):
        target, sem = refs[-2:]
        at = 0
        for piece in refs[: len(pieces)]:
            size = piece.shape[0]
            pltpu.make_async_copy(piece.at[:, lanes], target.at[at : at + size], sem).start()
            at += size
        pltpu.make_async_copy(target, target, sem).wait()

    return pl.pallas_call(
        kernel,
        in_specs=[FAR_SPEC] * len(pieces) + [SMEM_SPEC],
        out_specs=VMEM_SPEC,
        out_shape=pltpu.VMEM((width, features), BF16),
        scratch_shapes=[pltpu.SemaphoreType.DMA],
        compiler_params=pltpu.CompilerParams(vmem_limit_bytes=2**20),
        name="load_weight",
    )(*pieces, section)


def chunk_loop(weight_ref, body):
    lax.fori_loop(0, weight_ref.shape[0] // CHUNK, lambda i, c: (body(window(i)), c)[1], 0)


def wide_product(rows_ref, weight_ref, total_ref):
    total_ref[...] = jnp.zeros_like(total_ref)

    def body(w):
        total_ref[...] += plain_dot(rows_ref[:, w], weight_ref[w, :])

    chunk_loop(weight_ref, body)


def call(kernel, name, outs, operands, scratch=(), alias=None, limit=LIMIT):
    return pl.pallas_call(
        kernel,
        in_specs=[SMEM_SPEC] + [VMEM_SPEC] * (len(operands) - 1),
        out_shape=tuple(jax.ShapeDtypeStruct(shape, dtype) for shape, dtype in outs),
        out_specs=(VMEM_SPEC,) * len(outs),
        scratch_shapes=list(scratch),
        input_output_aliases=alias or {},
        compiler_params=pltpu.CompilerParams(vmem_limit_bytes=limit * 2**20),
        name=name,
    )(*operands)


def ahead(section, step, value, output, down_t, up, token, received):
    choices = [x for x in (token, received) if x is not None]
    rows, width = choices[0].shape
    features = up.shape[1]
    lowest, highest = (step - MICRO) // LAG + 1, step // LAG

    def kernel(section_ref, value_ref, output_ref, down_ref, up_ref, *refs):
        sources = refs[: len(choices)]
        next_ref, u_ref, low_ref, scale_ref = refs[len(choices) : len(choices) + 4]
        here = section_ref[0]

        def run(h_ref):
            wide = h_ref[...].astype(F32)
            scale = lax.rsqrt(jnp.mean(wide * wide, axis=-1, keepdims=True) + NORM_EPS)
            low = contract_trailing(h_ref[...], down_ref[...])
            scale_ref[...] = scale
            low_ref[...] = low
            low = (scale * low).astype(BF16)
            wide_product(h_ref, value_ref, u_ref)
            v = (scale * u_ref[...] + ADAPTER_SCALE * plain_dot(low, up_ref[...])).astype(BF16)

            def body(w):
                next_ref[:, w] = (
                    h_ref[:, w].astype(F32) + contract_trailing(v, output_ref[w, :])
                ).astype(BF16)

            chunk_loop(output_ref, body)

        @pl.when((here >= lowest) & (here <= highest) & (here < SECTIONS - 1))
        def _():
            if len(choices) == 1:
                run(sources[0])
            else:
                picked = refs[-1]
                picked[...] = jnp.where(here == 0, sources[0][...], sources[1][...])
                run(picked)

    return call(
        kernel,
        "ahead",
        [((rows, width), BF16), ((rows, features), F32), ((rows, ADAPTER_RANK), F32), ((rows, 1), F32)],
        [section, value, output, down_t, up] + choices,
        scratch=[pltpu.VMEM((rows, width), BF16)] * (len(choices) - 1),
    )


def add_gradients(down_acc, up_acc, hidden, scale, low, gv, gl):
    scaled = (scale * gl.astype(F32)).astype(BF16)
    down_acc[...] += contract_leading(scaled, hidden)
    low_rows = (scale * low).astype(BF16)
    up_acc[...] += ADAPTER_SCALE * contract_leading(low_rows, gv)


def gradient_pair(acc_ref, up_ref):
    gv = acc_ref[...].astype(BF16)
    return gv, (ADAPTER_SCALE * contract_trailing(gv, up_ref[...])).astype(BF16)


def reverse(section, value, output, down_t, up, grad, saved, grads, base):
    rows, width = grad.shape
    features = up.shape[1]
    owners = sorted(saved)
    flat = [x for s in owners for x in saved[s]]

    def kernel(section_ref, value_ref, output_ref, down_ref, up_ref, grad_ref, *refs):
        sets = {s: refs[4 * k : 4 * k + 4] for k, s in enumerate(owners)}
        prev_ref, down_acc, up_acc, acc_ref = refs[-4:]
        here = section_ref[0]

        def pick(k):
            x = sets[owners[0]][k][...]
            return x if len(owners) == 1 else jnp.where(here == owners[0], x, sets[owners[1]][k][...])

        def pick_window(w):
            x = sets[owners[0]][0][:, w]
            return x if len(owners) == 1 else jnp.where(here == owners[0], x, sets[owners[1]][0][:, w])

        @pl.when((here >= owners[0]) & (here <= owners[-1]))
        def _():
            wide_product(grad_ref, output_ref, acc_ref)
            gv, gl = gradient_pair(acc_ref, up_ref)
            u, low, scale = pick(1), pick(2), pick(3)
            centred = (
                jnp.sum(gv.astype(F32) * u, axis=-1, keepdims=True)
                + jnp.sum(gl.astype(F32) * low, axis=-1, keepdims=True)
            ) / width
            coef = scale * scale * scale * centred

            def body(w):
                grad_norm = contract_trailing(gv, value_ref[w, :]) + plain_dot(gl, down_ref[:, w])
                prev_ref[:, w] = (
                    grad_ref[:, w].astype(F32)
                    + scale * grad_norm
                    - pick_window(w).astype(F32) * coef
                ).astype(BF16)

            chunk_loop(value_ref, body)
            add_gradients(down_acc, up_acc, pick(0), scale, low, gv, gl)

    operands = [section, value, output, down_t, up, grad] + flat + list(grads)
    first = len(operands) - 2
    alias = {first: 1, first + 1: 2}
    if base is not None:
        alias[len(operands)] = 0
        operands.append(base)
    return call(
        kernel,
        "reverse",
        [((rows, width), BF16), (grads[0].shape, F32), (grads[1].shape, F32)],
        operands,
        scratch=[pltpu.VMEM((rows, features), F32)],
        alias=alias,
    )


def reverse_first(section, output, up, grad, token, low, scale, grads):
    rows, features = grad.shape[0], up.shape[1]

    def kernel(section_ref, output_ref, up_ref, grad_ref, token_ref, low_ref, scale_ref, *refs):
        down_acc, up_acc, acc_ref = refs[2:]

        @pl.when(section_ref[0] == 0)
        def _():
            wide_product(grad_ref, output_ref, acc_ref)
            gv, gl = gradient_pair(acc_ref, up_ref)
            add_gradients(down_acc, up_acc, token_ref[...], scale_ref[...], low_ref[...], gv, gl)

    operands = [section, output, up, grad, token, low, scale] + list(grads)
    first = len(operands) - 2
    return call(
        kernel,
        "reverse_first",
        [(grads[0].shape, F32), (grads[1].shape, F32)],
        operands,
        scratch=[pltpu.VMEM((rows, features), F32)],
        alias={first: 0, first + 1: 1},
    )


def prepare(section, value, output, down_t, up, grad):
    rows, width = grad.shape
    features = up.shape[1]

    def kernel(section_ref, value_ref, output_ref, down_ref, up_ref, grad_ref, norm_ref, gv_ref, gl_ref, acc_ref):
        @pl.when(section_ref[0] == SECTIONS - 1)
        def _():
            wide_product(grad_ref, output_ref, acc_ref)
            gv, gl = gradient_pair(acc_ref, up_ref)
            gv_ref[...] = gv
            gl_ref[...] = gl

            def body(w):
                norm_ref[:, w] = contract_trailing(gv, value_ref[w, :]) + plain_dot(gl, down_ref[:, w])

            chunk_loop(value_ref, body)

    return call(
        kernel,
        "prepare",
        [((rows, width), F32), ((rows, features), BF16), ((rows, ADAPTER_RANK), BF16)],
        [section, value, output, down_t, up, grad],
        scratch=[pltpu.VMEM((rows, features), F32)],
    )


def join_last(section, down_t, hidden, grad_norm, gv, gl, grad, grads):
    rows, width = hidden.shape

    def kernel(section_ref, down_ref, h_ref, norm_ref, gv_ref, gl_ref, grad_ref, *refs):
        prev_ref, down_acc, up_acc = refs[2:]

        @pl.when(section_ref[0] == SECTIONS - 1)
        def _():
            wide = h_ref[...].astype(F32)
            norm = norm_ref[...]
            low = contract_trailing(h_ref[...], down_ref[...])
            scale = lax.rsqrt(jnp.mean(wide * wide, axis=-1, keepdims=True) + NORM_EPS)
            centred = jnp.mean(wide * norm, axis=-1, keepdims=True)
            prev_ref[...] = (
                grad_ref[...].astype(F32) + scale * norm - wide * (scale * scale * scale * centred)
            ).astype(BF16)
            add_gradients(down_acc, up_acc, h_ref[...], scale, low, gv_ref[...], gl_ref[...])

    operands = [section, down_t, hidden, grad_norm, gv, gl, grad] + list(grads)
    first = len(operands) - 2
    return call(
        kernel,
        "join_last",
        [((rows, width), BF16), (grads[0].shape, F32), (grads[1].shape, F32)],
        operands,
        alias={first: 1, first + 1: 2},
    )


def reorder_kernel(place_ref, tokens_ref, grads_ref, *refs):
    targets, sem = refs[: 2 * MICRO], refs[-1]
    rows = targets[0].shape[0]
    block = tokens_ref.shape[1] // place_ref.shape[0]

    def copy_of(slot, k):
        source = (tokens_ref, grads_ref)[k // MICRO]
        m = k % MICRO
        origin = pl.multiple_of(place_ref[slot] * block, block)
        goal = pl.multiple_of(slot * block, block)
        return pltpu.make_async_copy(
            source.at[m * rows : (m + 1) * rows, pl.ds(origin, block)],
            targets[k].at[:, pl.ds(goal, block)],
            sem.at[k],
        )

    def begin(slot, carry):
        for k in range(2 * MICRO):
            copy_of(slot, k).start()
        return carry

    lax.fori_loop(0, place_ref.shape[0], begin, 0)
    for k in range(2 * MICRO):
        pltpu.make_async_copy(targets[k], targets[k], sem.at[k]).wait()


def reorder(place, tokens, grads):
    rows = tokens.shape[0] // MICRO
    return pl.pallas_call(
        reorder_kernel,
        in_specs=[pl.BlockSpec(memory_space=pltpu.SMEM), FAR_SPEC, FAR_SPEC],
        out_specs=(FAR_SPEC,) * (2 * MICRO),
        out_shape=(jax.ShapeDtypeStruct((rows, tokens.shape[1]), BF16),) * (2 * MICRO),
        scratch_shapes=[pltpu.SemaphoreType.DMA((2 * MICRO,))],
        compiler_params=pltpu.CompilerParams(vmem_limit_bytes=2**20),
        name="reorder",
    )(place, tokens, grads)


def torus_shift(first, by):
    pairs = []
    for y in range(RING):
        for z in range(RING):
            for core in range(2):
                along_y = (core == 0) == first
                ty, tz = ((y + by) % RING, z) if along_y else (y, (z + by) % RING)
                pairs.append(((y * RING + z) * 2 + core, (ty * RING + tz) * 2 + core))
    return pairs


def ring_pieces(head, tail, first, between=lambda x: x):
    up_pairs, down_pairs = torus_shift(first, 1), torus_shift(first, -1)
    before_head = lax.ppermute(head, "dp", up_pairs)
    after_tail = lax.ppermute(tail, "dp", down_pairs)
    before_tail = lax.ppermute(tail, "dp", up_pairs)
    after_head = lax.ppermute(head, "dp", down_pairs)
    before_head, after_tail = between((before_head, after_tail))
    far_head = lax.ppermute(before_head, "dp", up_pairs)
    far_tail = lax.ppermute(after_tail, "dp", down_pairs)
    return [head, tail, before_head, before_tail, after_head, after_tail, far_head, far_tail]


def near_groups(block):
    half = block.shape[0] // 2
    near = ring_pieces(block[:half], block[half:], True)
    return jnp.concatenate(near[:4], axis=0), jnp.concatenate(near[4:], axis=0)


def far_pieces(group_head, group_tail, between):
    mine = ring_pieces(group_head, group_tail, False, between)
    swap = [(i, i ^ 1) for i in range(2 * RING * RING)]
    pieces = mine + [lax.ppermute(piece, "dp", swap) for piece in mine]
    return [pltpu.with_memory_space_constraint(piece, pltpu.HBM) for piece in pieces]


def slot_places(owner_index):
    offsets = jnp.array([0, -1, 1, 2], jnp.int32)
    core = owner_index % 2
    chip = owner_index // 2
    y, z = chip // RING, chip % RING
    outer = jnp.repeat(offsets, RING)
    inner = jnp.tile(offsets, RING)
    by_y = ((y + inner) % RING * RING + (z + outer) % RING) * 2
    by_z = ((y + outer) % RING * RING + (z + inner) % RING) * 2 + 1
    return jnp.where(core == 0, jnp.concatenate([by_y, by_z]), jnp.concatenate([by_z, by_y]))


def adam_update(params_old, first_old, second_old, slot_grad, live):
    first_step = BETA_FIRST * first_old + (1.0 - BETA_FIRST) * slot_grad
    second_step = BETA_SECOND * second_old + (1.0 - BETA_SECOND) * slot_grad * slot_grad
    step_size = first_step / FIRST_FIX / (jnp.sqrt(second_step / SECOND_FIX) + ADAM_EPS)
    params_step = (params_old.astype(jnp.float32) - LEARN_RATE * step_size).astype(jnp.bfloat16)
    return (
        jnp.where(live, params_step, params_old),
        jnp.where(live, first_step, first_old),
        jnp.where(live, second_step, second_old),
    )


def on_device(
    tokens,
    cotangent,
    gains,
    value_projection_weight,
    output_projection_weight,
    block_adapter_ids,
    job_adapter,
    job_slab,
    token_counts,
    slot_adapter_params,
    first_moment,
    second_moment,
):
    section_index = lax.axis_index("section")
    owner_index = lax.axis_index("dp")
    section_total = lax.axis_size("section")
    owner_total = lax.axis_size("dp")
    tok_dev, hidden_width = tokens.shape
    value_feature_width = value_projection_weight.shape[2]
    panel_width = slot_adapter_params.shape[2]
    slab_count = owner_total // 2
    block_total = block_adapter_ids.shape[0]
    local_blocks = block_total // owner_total
    block_rows = tok_dev // local_blocks
    adapter_total = token_counts.shape[0]
    divide_position = hidden_width * ADAPTER_RANK
    gain_row = gains[0]
    shard_rows = value_projection_weight.shape[1]
    my_gain = lax.dynamic_slice_in_dim(gain_row, owner_index * shard_rows, shard_rows)
    scaled_value = (value_projection_weight[0].astype(F32) * my_gain[:, None]).astype(BF16)
    my_jobs = lax.dynamic_index_in_dim(job_adapter, owner_index, 0, keepdims=False)
    my_blocks = lax.dynamic_slice_in_dim(
        block_adapter_ids, owner_index * local_blocks, local_blocks
    )
    slab_ids = jnp.arange(slab_count, dtype=jnp.int32)
    matching = (job_adapter[None, None] == my_blocks[:, None, None, None]) & (
        job_slab[None, None] == slab_ids[None, :, None, None]
    )
    owner_ids = jnp.arange(owner_total, dtype=jnp.int32)
    source_owner = jnp.sum(jnp.where(matching, owner_ids[None, None, :, None], 0), axis=(2, 3))
    own_select = (block_adapter_ids[:, None] == my_jobs[None, :]) & (my_jobs[None, :] >= 0)
    slot_rows = jnp.arange(local_blocks, dtype=jnp.int32)[:, None]

    def hand_out(owned):
        picked = jnp.dot(own_select.astype(jnp.bfloat16), owned, preferred_element_type=jnp.float32)
        return picked.astype(jnp.bfloat16).reshape(owner_total, local_blocks, panel_width)

    def assemble(arrived):
        gathered_slabs = arrived[source_owner, slot_rows]
        return gathered_slabs.reshape(local_blocks, slab_count * panel_width)

    arrived_panels = lax.all_to_all(
        hand_out(slot_adapter_params[0]), "dp", split_axis=0, concat_axis=0, tiled=True
    )
    blocks_of = lambda flat: flat.reshape(owner_total, -1)

    def set_up(inputs):
        panels, tokens, cotangent, gain_row, places = inputs
        reordered = reorder(places, tokens, cotangent)
        token_micro, cot_micro = list(reordered[:MICRO]), list(reordered[MICRO:])
        gathered = assemble(panels)
        gain_slots = blocks_of(gain_row)[places].reshape(-1)
        down_t = (
            blocks_of(gathered[0, :divide_position])[places]
            .reshape(hidden_width, ADAPTER_RANK)
            .T.astype(F32)
            * gain_slots[None, :]
        ).astype(BF16)
        up = gathered[0, divide_position:].reshape(ADAPTER_RANK, value_feature_width)
        return token_micro, cot_micro, gain_slots, down_t, up

    inputs = (arrived_panels, tokens, cotangent, gain_row, slot_places(owner_index))
    block = jnp.concatenate([scaled_value, output_projection_weight[0]], axis=1)
    group_head, group_tail = near_groups(block)
    group_head, group_tail, inputs = lax.optimization_barrier((group_head, group_tail, inputs))
    places = inputs[-1]
    ready = set_up(inputs)
    kept = []

    def between(arrived):
        arrived, early = lax.optimization_barrier((arrived, ready))
        kept.append(early)
        return arrived

    pieces = far_pieces(group_head, group_tail, between)
    token_micro, cot_micro, gain_slots, down_t, up = kept[0]
    prepared = []
    last = section_total - 1
    ahead_pairs = [(i, i + 1) for i in range(last)]
    back_pairs = [(i + 1, i) for i in range(last)]
    section = jnp.full((1,), section_index, jnp.int32)
    grads = (
        jnp.zeros((ADAPTER_RANK, hidden_width), F32),
        jnp.zeros((ADAPTER_RANK, value_feature_width), F32),
    )
    section, grads, token_micro = lax.optimization_barrier((section, grads, token_micro))
    value = load_weight(pieces, slice(0, value_feature_width), section)
    output = load_weight(
        pieces, slice(value_feature_width, 2 * value_feature_width), section
    )

    entering, ahead_state, ahead_sent, back_sent = {}, {}, {}, {}
    for step in range(2 * last * LAG + MICRO):
        if step - LAG in ahead_sent:
            entering[step] = ahead_sent[step - LAG]
        if step < (last - 1) * LAG + MICRO:
            token = token_micro[step] if step < MICRO else None
            result = ahead(section, step, value, output, down_t, up, token, entering.get(step))
            ahead_state[step] = result[1:]
            ahead_sent[step] = lax.ppermute(result[0], "section", ahead_pairs)
        if step < MICRO:
            done = prepare(section, value, output, down_t, up, cot_micro[step])
            section, *done = lax.optimization_barrier((section,) + tuple(done))
            prepared.append(done)
        incoming = back_sent.get(step - LAG)
        m = step - LAG * last
        outgoing_rows = None
        if 0 <= m < MICRO:
            norm, gv, gl = prepared[m]
            outgoing_rows, *grads = join_last(
                section, down_t, entering[step], norm, gv, gl, cot_micro[m], grads
            )
        saved = {}
        for s in range(1, last):
            m = step - LAG * (2 * last - s)
            if 0 <= m < MICRO:
                saved[s] = (entering[LAG * s + m],) + tuple(ahead_state[LAG * s + m])
        if saved:
            back, *grads = reverse(section, value, output, down_t, up, incoming, saved, grads, outgoing_rows)
            outgoing_rows = back
        if outgoing_rows is not None:
            back_sent[step] = lax.ppermute(outgoing_rows, "section", back_pairs)
        m = step - LAG * 2 * last
        if 0 <= m < MICRO:
            _, low, scale = ahead_state[m]
            grads = reverse_first(
                section, output, up, incoming, token_micro[m], low, scale, grads
            )

    natural = jnp.sum(
        jnp.where(places[None, :] == owner_ids[:, None], owner_ids[None, :], 0), axis=1
    )
    down_grad = (grads[0] * gain_slots[None, :]).astype(BF16).T
    block_grads = jnp.concatenate(
        [blocks_of(down_grad)[natural].reshape(-1), grads[1].astype(BF16).reshape(-1)]
    )
    outgoing = (
        jnp.zeros((owner_total, local_blocks, panel_width), BF16)
        .at[source_owner, slot_rows]
        .set(block_grads.reshape(local_blocks, slab_count, panel_width))
    )
    arrived = lax.all_to_all(outgoing, "dp", split_axis=0, concat_axis=0, tiled=True)
    summed = jnp.dot(
        own_select.astype(BF16).T,
        arrived.reshape(block_total, panel_width),
        preferred_element_type=F32,
    )
    live = my_jobs >= 0
    adapter_ids = jnp.arange(adapter_total, dtype=jnp.int32)
    slot_counts = jnp.sum(
        jnp.where(adapter_ids[None, :] == my_jobs[:, None], token_counts[None, :], 0), axis=1
    )
    slot_counts = jnp.where(live, slot_counts, 1)
    slot_grad = summed / slot_counts.astype(jnp.float32)[:, None]
    params_new, first_new, second_new = adam_update(
        slot_adapter_params[0], first_moment[0], second_moment[0], slot_grad, live[:, None]
    )
    returned = assemble(
        lax.all_to_all(hand_out(params_new), "dp", split_axis=0, concat_axis=0, tiled=True)
    )
    return (params_new[None], first_new[None], second_new[None], returned[None])


def solution(mesh):
    return jax.shard_map(
        on_device,
        mesh=mesh,
        in_specs=(
            P("dp", None),
            P("dp", None),
            P("section", None),
            P("section", "dp", None),
            P("section", "dp", None),
            P(),
            P(),
            P(),
            P(),
            P("section", "dp", None),
            P("section", "dp", None),
            P("section", "dp", None),
        ),
        out_specs=(
            P("section", "dp", None),
            P("section", "dp", None),
            P("section", "dp", None),
            P("section", "dp", None),
        ),
        check_vma=False,
    )
```

```python
import jax
import jax.numpy as jnp
from jax import lax
from jax.experimental import pallas as pl
from jax.experimental.pallas import tpu as pltpu
from jax.sharding import PartitionSpec as P

ADAPTER_RANK = 16
MICRO = 4
LIMIT = 4
SECTIONS = 4
LAG = 2
CHUNK = 1024
RING = 4

ADAPTER_SCALE = 2.0
LEARN_RATE = 0.001
BETA_FIRST = 0.9
BETA_SECOND = 0.999
ADAM_EPS = 1e-08
FIRST_FIX = 1.0 - 0.9**50 * 0.9**50
SECOND_FIX = 1.0 - 0.999**50 * 0.999**50
NORM_EPS = 1e-05
F32 = jnp.float32
BF16 = jnp.bfloat16


def contract_trailing(left, right):
    return lax.dot_general(
        left, right, (((1,), (1,)), ((), ())), preferred_element_type=F32
    )


def contract_leading(left, right):
    return lax.dot_general(
        left, right, (((0,), (0,)), ((), ())), preferred_element_type=F32
    )


def plain_dot(left, right):
    return jnp.dot(left, right, preferred_element_type=F32)


def window(i):
    return pl.ds(pl.multiple_of(i * CHUNK, CHUNK), CHUNK)


VMEM_SPEC = pl.BlockSpec(memory_space=pltpu.VMEM)
SMEM_SPEC = pl.BlockSpec(memory_space=pltpu.SMEM)
FAR_SPEC = pl.BlockSpec(memory_space=pltpu.HBM)


def load_weight(pieces, chosen, lanes, section, base=None):
    features = lanes.stop - lanes.start
    sizes = [piece.shape[0] for piece in pieces]
    taken = [pieces[k] for k in chosen]
    rest = [] if base is None else [base]

    def kernel(*refs):
        target, sem = refs[-2:]
        for k, piece in zip(chosen, refs[: len(chosen)]):
            at = sum(sizes[:k])
            pltpu.make_async_copy(
                piece.at[:, lanes], target.at[at : at + sizes[k]], sem
            ).start()
        moved = target.at[0 : sum(sizes[k] for k in chosen)]
        pltpu.make_async_copy(moved, moved, sem).wait()

    return pl.pallas_call(
        kernel,
        in_specs=[FAR_SPEC] * len(taken) + [SMEM_SPEC] + [VMEM_SPEC] * len(rest),
        out_specs=VMEM_SPEC,
        out_shape=pltpu.VMEM((sum(sizes), features), BF16),
        scratch_shapes=[pltpu.SemaphoreType.DMA],
        input_output_aliases={len(taken) + 1: 0} if rest else {},
        compiler_params=pltpu.CompilerParams(vmem_limit_bytes=2**20),
        name="load_weight",
    )(*taken, section, *rest)


def chunk_loop(weight_ref, body):
    lax.fori_loop(0, weight_ref.shape[0] // CHUNK, lambda i, c: (body(window(i)), c)[1], 0)


def wide_product(rows_ref, weight_ref, total_ref):
    total_ref[...] = jnp.zeros_like(total_ref)

    def body(w):
        total_ref[...] += plain_dot(rows_ref[:, w], weight_ref[w, :])

    chunk_loop(weight_ref, body)


def call(kernel, name, outs, operands, scratch=(), alias=None, limit=LIMIT):
    return pl.pallas_call(
        kernel,
        in_specs=[SMEM_SPEC] + [VMEM_SPEC] * (len(operands) - 1),
        out_shape=tuple(jax.ShapeDtypeStruct(shape, dtype) for shape, dtype in outs),
        out_specs=(VMEM_SPEC,) * len(outs),
        scratch_shapes=list(scratch),
        input_output_aliases=alias or {},
        compiler_params=pltpu.CompilerParams(vmem_limit_bytes=limit * 2**20),
        name=name,
    )(*operands)


def ahead(section, step, value, output, down_t, up, token, received):
    choices = [x for x in (token, received) if x is not None]
    rows, width = choices[0].shape
    features = up.shape[1]
    lowest, highest = (step - MICRO) // LAG + 1, step // LAG

    def kernel(section_ref, value_ref, output_ref, down_ref, up_ref, *refs):
        sources = refs[: len(choices)]
        next_ref, u_ref, low_ref, scale_ref = refs[len(choices) : len(choices) + 4]
        here = section_ref[0]

        def run(h_ref):
            wide = h_ref[...].astype(F32)
            scale = lax.rsqrt(jnp.mean(wide * wide, axis=-1, keepdims=True) + NORM_EPS)
            low = contract_trailing(h_ref[...], down_ref[...])
            scale_ref[...] = scale
            low_ref[...] = low
            low = (scale * low).astype(BF16)
            wide_product(h_ref, value_ref, u_ref)
            v = (scale * u_ref[...] + ADAPTER_SCALE * plain_dot(low, up_ref[...])).astype(BF16)

            def body(w):
                next_ref[:, w] = (
                    h_ref[:, w].astype(F32) + contract_trailing(v, output_ref[w, :])
                ).astype(BF16)

            chunk_loop(output_ref, body)

        @pl.when((here >= lowest) & (here <= highest) & (here < SECTIONS - 1))
        def _():
            if len(choices) == 1:
                run(sources[0])
            else:
                picked = refs[-1]
                picked[...] = jnp.where(here == 0, sources[0][...], sources[1][...])
                run(picked)

    return call(
        kernel,
        "ahead",
        [((rows, width), BF16), ((rows, features), F32), ((rows, ADAPTER_RANK), F32), ((rows, 1), F32)],
        [section, value, output, down_t, up] + choices,
        scratch=[pltpu.VMEM((rows, width), BF16)] * (len(choices) - 1),
    )


def add_gradients(down_acc, up_acc, hidden, scale, low, gv, gl):
    scaled = (scale * gl.astype(F32)).astype(BF16)
    down_acc[...] += contract_leading(scaled, hidden)
    low_rows = (scale * low).astype(BF16)
    up_acc[...] += ADAPTER_SCALE * contract_leading(low_rows, gv)


def gradient_pair(acc_ref, up_ref):
    gv = acc_ref[...].astype(BF16)
    return gv, (ADAPTER_SCALE * contract_trailing(gv, up_ref[...])).astype(BF16)


def reverse(section, value, output, down_t, up, grad, saved, grads, base):
    rows, width = grad.shape
    features = up.shape[1]
    owners = sorted(saved)
    flat = [x for s in owners for x in saved[s]]

    def kernel(section_ref, value_ref, output_ref, down_ref, up_ref, grad_ref, *refs):
        sets = {s: refs[4 * k : 4 * k + 4] for k, s in enumerate(owners)}
        prev_ref, down_acc, up_acc, acc_ref = refs[-4:]
        here = section_ref[0]

        def pick(k):
            x = sets[owners[0]][k][...]
            return x if len(owners) == 1 else jnp.where(here == owners[0], x, sets[owners[1]][k][...])

        def pick_window(w):
            x = sets[owners[0]][0][:, w]
            return x if len(owners) == 1 else jnp.where(here == owners[0], x, sets[owners[1]][0][:, w])

        @pl.when((here >= owners[0]) & (here <= owners[-1]))
        def _():
            wide_product(grad_ref, output_ref, acc_ref)
            gv, gl = gradient_pair(acc_ref, up_ref)
            u, low, scale = pick(1), pick(2), pick(3)
            centred = (
                jnp.sum(gv.astype(F32) * u, axis=-1, keepdims=True)
                + jnp.sum(gl.astype(F32) * low, axis=-1, keepdims=True)
            ) / width
            coef = scale * scale * scale * centred

            def body(w):
                grad_norm = contract_trailing(gv, value_ref[w, :]) + plain_dot(gl, down_ref[:, w])
                prev_ref[:, w] = (
                    grad_ref[:, w].astype(F32)
                    + scale * grad_norm
                    - pick_window(w).astype(F32) * coef
                ).astype(BF16)

            chunk_loop(value_ref, body)
            add_gradients(down_acc, up_acc, pick(0), scale, low, gv, gl)

    operands = [section, value, output, down_t, up, grad] + flat + list(grads)
    first = len(operands) - 2
    alias = {first: 1, first + 1: 2}
    if base is not None:
        alias[len(operands)] = 0
        operands.append(base)
    return call(
        kernel,
        "reverse",
        [((rows, width), BF16), (grads[0].shape, F32), (grads[1].shape, F32)],
        operands,
        scratch=[pltpu.VMEM((rows, features), F32)],
        alias=alias,
    )


def reverse_first(section, output, up, grad, token, low, scale, grads):
    rows, features = grad.shape[0], up.shape[1]

    def kernel(section_ref, output_ref, up_ref, grad_ref, token_ref, low_ref, scale_ref, *refs):
        down_acc, up_acc, acc_ref = refs[2:]

        @pl.when(section_ref[0] == 0)
        def _():
            wide_product(grad_ref, output_ref, acc_ref)
            gv, gl = gradient_pair(acc_ref, up_ref)
            add_gradients(down_acc, up_acc, token_ref[...], scale_ref[...], low_ref[...], gv, gl)

    operands = [section, output, up, grad, token, low, scale] + list(grads)
    first = len(operands) - 2
    return call(
        kernel,
        "reverse_first",
        [(grads[0].shape, F32), (grads[1].shape, F32)],
        operands,
        scratch=[pltpu.VMEM((rows, features), F32)],
        alias={first: 0, first + 1: 1},
    )


def prepare(section, value, output, down_t, up, grad):
    rows, width = grad.shape
    features = up.shape[1]

    def kernel(section_ref, value_ref, output_ref, down_ref, up_ref, grad_ref, norm_ref, gv_ref, gl_ref, acc_ref):
        @pl.when(section_ref[0] == SECTIONS - 1)
        def _():
            wide_product(grad_ref, output_ref, acc_ref)
            gv, gl = gradient_pair(acc_ref, up_ref)
            gv_ref[...] = gv
            gl_ref[...] = gl

            def body(w):
                norm_ref[:, w] = contract_trailing(gv, value_ref[w, :]) + plain_dot(gl, down_ref[:, w])

            chunk_loop(value_ref, body)

    return call(
        kernel,
        "prepare",
        [((rows, width), F32), ((rows, features), BF16), ((rows, ADAPTER_RANK), BF16)],
        [section, value, output, down_t, up, grad],
        scratch=[pltpu.VMEM((rows, features), F32)],
    )


def join_last(section, down_t, hidden, grad_norm, gv, gl, grad, grads):
    rows, width = hidden.shape

    def kernel(section_ref, down_ref, h_ref, norm_ref, gv_ref, gl_ref, grad_ref, *refs):
        prev_ref, down_acc, up_acc = refs[2:]

        @pl.when(section_ref[0] == SECTIONS - 1)
        def _():
            wide = h_ref[...].astype(F32)
            norm = norm_ref[...]
            low = contract_trailing(h_ref[...], down_ref[...])
            scale = lax.rsqrt(jnp.mean(wide * wide, axis=-1, keepdims=True) + NORM_EPS)
            centred = jnp.mean(wide * norm, axis=-1, keepdims=True)
            prev_ref[...] = (
                grad_ref[...].astype(F32) + scale * norm - wide * (scale * scale * scale * centred)
            ).astype(BF16)
            add_gradients(down_acc, up_acc, h_ref[...], scale, low, gv_ref[...], gl_ref[...])

    operands = [section, down_t, hidden, grad_norm, gv, gl, grad] + list(grads)
    first = len(operands) - 2
    return call(
        kernel,
        "join_last",
        [((rows, width), BF16), (grads[0].shape, F32), (grads[1].shape, F32)],
        operands,
        alias={first: 1, first + 1: 2},
    )


def reorder_kernel(place_ref, tokens_ref, grads_ref, *refs):
    targets, sem = refs[: 2 * MICRO], refs[-1]
    rows = targets[0].shape[0]
    block = tokens_ref.shape[1] // place_ref.shape[0]

    def copy_of(slot, k):
        source = (tokens_ref, grads_ref)[k // MICRO]
        m = k % MICRO
        origin = pl.multiple_of(place_ref[slot] * block, block)
        goal = pl.multiple_of(slot * block, block)
        return pltpu.make_async_copy(
            source.at[m * rows : (m + 1) * rows, pl.ds(origin, block)],
            targets[k].at[:, pl.ds(goal, block)],
            sem.at[k],
        )

    def begin(slot, carry):
        for k in range(2 * MICRO):
            copy_of(slot, k).start()
        return carry

    lax.fori_loop(0, place_ref.shape[0], begin, 0)
    for k in range(2 * MICRO):
        pltpu.make_async_copy(targets[k], targets[k], sem.at[k]).wait()


def reorder(place, tokens, grads):
    rows = tokens.shape[0] // MICRO
    return pl.pallas_call(
        reorder_kernel,
        in_specs=[pl.BlockSpec(memory_space=pltpu.SMEM), FAR_SPEC, FAR_SPEC],
        out_specs=(FAR_SPEC,) * (2 * MICRO),
        out_shape=(jax.ShapeDtypeStruct((rows, tokens.shape[1]), BF16),) * (2 * MICRO),
        scratch_shapes=[pltpu.SemaphoreType.DMA((2 * MICRO,))],
        compiler_params=pltpu.CompilerParams(vmem_limit_bytes=2**20),
        name="reorder",
    )(place, tokens, grads)


def torus_shift(first, by):
    pairs = []
    for y in range(RING):
        for z in range(RING):
            for core in range(2):
                along_y = (core == 0) == first
                ty, tz = ((y + by) % RING, z) if along_y else (y, (z + by) % RING)
                pairs.append(((y * RING + z) * 2 + core, (ty * RING + tz) * 2 + core))
    return pairs


def ring_pieces(head, tail, first, between=lambda x: x):
    up_pairs, down_pairs = torus_shift(first, 1), torus_shift(first, -1)
    before_head = lax.ppermute(head, "dp", up_pairs)
    after_tail = lax.ppermute(tail, "dp", down_pairs)
    before_tail = lax.ppermute(tail, "dp", up_pairs)
    after_head = lax.ppermute(head, "dp", down_pairs)
    before_head, after_tail = between((before_head, after_tail))
    far_head = lax.ppermute(before_head, "dp", up_pairs)
    far_tail = lax.ppermute(after_tail, "dp", down_pairs)
    return [head, tail, before_head, before_tail, after_head, after_tail, far_head, far_tail]


def near_groups(block):
    half = block.shape[0] // 2
    near = ring_pieces(block[:half], block[half:], True)
    return jnp.concatenate(near[:4], axis=0), jnp.concatenate(near[4:], axis=0)


def far_pieces(group_head, group_tail, between):
    mine = ring_pieces(group_head, group_tail, False, between)
    swap = [(i, i ^ 1) for i in range(2 * RING * RING)]
    pieces = mine + [lax.ppermute(piece, "dp", swap) for piece in mine]
    return [pltpu.with_memory_space_constraint(piece, pltpu.HBM) for piece in pieces]


def slot_places(owner_index):
    offsets = jnp.array([0, -1, 1, 2], jnp.int32)
    core = owner_index % 2
    chip = owner_index // 2
    y, z = chip // RING, chip % RING
    outer = jnp.repeat(offsets, RING)
    inner = jnp.tile(offsets, RING)
    by_y = ((y + inner) % RING * RING + (z + outer) % RING) * 2
    by_z = ((y + outer) % RING * RING + (z + inner) % RING) * 2 + 1
    return jnp.where(core == 0, jnp.concatenate([by_y, by_z]), jnp.concatenate([by_z, by_y]))


def adam_update(params_old, first_old, second_old, slot_grad, live):
    first_step = BETA_FIRST * first_old + (1.0 - BETA_FIRST) * slot_grad
    second_step = BETA_SECOND * second_old + (1.0 - BETA_SECOND) * slot_grad * slot_grad
    step_size = first_step / FIRST_FIX / (jnp.sqrt(second_step / SECOND_FIX) + ADAM_EPS)
    params_step = (params_old.astype(jnp.float32) - LEARN_RATE * step_size).astype(jnp.bfloat16)
    return (
        jnp.where(live, params_step, params_old),
        jnp.where(live, first_step, first_old),
        jnp.where(live, second_step, second_old),
    )


def on_device(
    tokens,
    cotangent,
    gains,
    value_projection_weight,
    output_projection_weight,
    block_adapter_ids,
    job_adapter,
    job_slab,
    token_counts,
    slot_adapter_params,
    first_moment,
    second_moment,
):
    section_index = lax.axis_index("section")
    owner_index = lax.axis_index("dp")
    section_total = lax.axis_size("section")
    owner_total = lax.axis_size("dp")
    tok_dev, hidden_width = tokens.shape
    value_feature_width = value_projection_weight.shape[2]
    panel_width = slot_adapter_params.shape[2]
    slab_count = owner_total // 2
    block_total = block_adapter_ids.shape[0]
    local_blocks = block_total // owner_total
    block_rows = tok_dev // local_blocks
    adapter_total = token_counts.shape[0]
    divide_position = hidden_width * ADAPTER_RANK
    gain_row = gains[0]
    shard_rows = value_projection_weight.shape[1]
    my_gain = lax.dynamic_slice_in_dim(gain_row, owner_index * shard_rows, shard_rows)
    scaled_value = (value_projection_weight[0].astype(F32) * my_gain[:, None]).astype(BF16)
    my_jobs = lax.dynamic_index_in_dim(job_adapter, owner_index, 0, keepdims=False)
    my_blocks = lax.dynamic_slice_in_dim(
        block_adapter_ids, owner_index * local_blocks, local_blocks
    )
    slab_ids = jnp.arange(slab_count, dtype=jnp.int32)
    matching = (job_adapter[None, None] == my_blocks[:, None, None, None]) & (
        job_slab[None, None] == slab_ids[None, :, None, None]
    )
    owner_ids = jnp.arange(owner_total, dtype=jnp.int32)
    source_owner = jnp.sum(jnp.where(matching, owner_ids[None, None, :, None], 0), axis=(2, 3))
    own_select = (block_adapter_ids[:, None] == my_jobs[None, :]) & (my_jobs[None, :] >= 0)
    slot_rows = jnp.arange(local_blocks, dtype=jnp.int32)[:, None]

    def hand_out(owned):
        picked = jnp.dot(own_select.astype(jnp.bfloat16), owned, preferred_element_type=jnp.float32)
        return picked.astype(jnp.bfloat16).reshape(owner_total, local_blocks, panel_width)

    def assemble(arrived):
        gathered_slabs = arrived[source_owner, slot_rows]
        return gathered_slabs.reshape(local_blocks, slab_count * panel_width)

    arrived_panels = lax.all_to_all(
        hand_out(slot_adapter_params[0]), "dp", split_axis=0, concat_axis=0, tiled=True
    )
    blocks_of = lambda flat: flat.reshape(owner_total, -1)

    def set_up(inputs):
        panels, tokens, cotangent, gain_row, places = inputs
        reordered = reorder(places, tokens, cotangent)
        token_micro, cot_micro = list(reordered[:MICRO]), list(reordered[MICRO:])
        gathered = assemble(panels)
        gain_slots = blocks_of(gain_row)[places].reshape(-1)
        down_t = (
            blocks_of(gathered[0, :divide_position])[places]
            .reshape(hidden_width, ADAPTER_RANK)
            .T.astype(F32)
            * gain_slots[None, :]
        ).astype(BF16)
        up = gathered[0, divide_position:].reshape(ADAPTER_RANK, value_feature_width)
        return token_micro, cot_micro, gain_slots, down_t, up

    inputs = (arrived_panels, tokens, cotangent, gain_row, slot_places(owner_index))
    block = jnp.concatenate([scaled_value, output_projection_weight[0]], axis=1)
    group_head, group_tail = near_groups(block)
    group_head, group_tail, inputs = lax.optimization_barrier((group_head, group_tail, inputs))
    places = inputs[-1]
    ready = set_up(inputs)
    kept = []

    def between(arrived):
        arrived, early = lax.optimization_barrier((arrived, ready))
        kept.append(early)
        return arrived

    pieces = far_pieces(group_head, group_tail, between)
    token_micro, cot_micro, gain_slots, down_t, up = kept[0]
    prepared = []
    last = section_total - 1
    ahead_pairs = [(i, i + 1) for i in range(last)]
    back_pairs = [(i + 1, i) for i in range(last)]
    section = jnp.full((1,), section_index, jnp.int32)
    grads = (
        jnp.zeros((ADAPTER_RANK, hidden_width), F32),
        jnp.zeros((ADAPTER_RANK, value_feature_width), F32),
    )
    section, grads, token_micro = lax.optimization_barrier((section, grads, token_micro))
    early, late = range(len(pieces) - 2), range(len(pieces) - 2, len(pieces))
    value_lanes = slice(0, value_feature_width)
    output_lanes = slice(value_feature_width, 2 * value_feature_width)
    value = load_weight(pieces, early, value_lanes, section)
    output = load_weight(pieces, early, output_lanes, section)
    value = load_weight(pieces, late, value_lanes, section, value)
    output = load_weight(pieces, late, output_lanes, section, output)

    entering, ahead_state, ahead_sent, back_sent = {}, {}, {}, {}
    for step in range(2 * last * LAG + MICRO):
        if step - LAG in ahead_sent:
            entering[step] = ahead_sent[step - LAG]
        if step < (last - 1) * LAG + MICRO:
            token = token_micro[step] if step < MICRO else None
            result = ahead(section, step, value, output, down_t, up, token, entering.get(step))
            ahead_state[step] = result[1:]
            ahead_sent[step] = lax.ppermute(result[0], "section", ahead_pairs)
        if step < MICRO:
            done = prepare(section, value, output, down_t, up, cot_micro[step])
            section, *done = lax.optimization_barrier((section,) + tuple(done))
            prepared.append(done)
        incoming = back_sent.get(step - LAG)
        m = step - LAG * last
        outgoing_rows = None
        if 0 <= m < MICRO:
            norm, gv, gl = prepared[m]
            outgoing_rows, *grads = join_last(
                section, down_t, entering[step], norm, gv, gl, cot_micro[m], grads
            )
        saved = {}
        for s in range(1, last):
            m = step - LAG * (2 * last - s)
            if 0 <= m < MICRO:
                saved[s] = (entering[LAG * s + m],) + tuple(ahead_state[LAG * s + m])
        if saved:
            back, *grads = reverse(section, value, output, down_t, up, incoming, saved, grads, outgoing_rows)
            outgoing_rows = back
        if outgoing_rows is not None:
            back_sent[step] = lax.ppermute(outgoing_rows, "section", back_pairs)
        m = step - LAG * 2 * last
        if 0 <= m < MICRO:
            _, low, scale = ahead_state[m]
            grads = reverse_first(
                section, output, up, incoming, token_micro[m], low, scale, grads
            )

    natural = jnp.sum(
        jnp.where(places[None, :] == owner_ids[:, None], owner_ids[None, :], 0), axis=1
    )
    down_grad = (grads[0] * gain_slots[None, :]).astype(BF16).T
    block_grads = jnp.concatenate(
        [blocks_of(down_grad)[natural].reshape(-1), grads[1].astype(BF16).reshape(-1)]
    )
    outgoing = (
        jnp.zeros((owner_total, local_blocks, panel_width), BF16)
        .at[source_owner, slot_rows]
        .set(block_grads.reshape(local_blocks, slab_count, panel_width))
    )
    arrived = lax.all_to_all(outgoing, "dp", split_axis=0, concat_axis=0, tiled=True)
    summed = jnp.dot(
        own_select.astype(BF16).T,
        arrived.reshape(block_total, panel_width),
        preferred_element_type=F32,
    )
    live = my_jobs >= 0
    adapter_ids = jnp.arange(adapter_total, dtype=jnp.int32)
    slot_counts = jnp.sum(
        jnp.where(adapter_ids[None, :] == my_jobs[:, None], token_counts[None, :], 0), axis=1
    )
    slot_counts = jnp.where(live, slot_counts, 1)
    slot_grad = summed / slot_counts.astype(jnp.float32)[:, None]
    params_new, first_new, second_new = adam_update(
        slot_adapter_params[0], first_moment[0], second_moment[0], slot_grad, live[:, None]
    )
    returned = assemble(
        lax.all_to_all(hand_out(params_new), "dp", split_axis=0, concat_axis=0, tiled=True)
    )
    return (params_new[None], first_new[None], second_new[None], returned[None])


def solution(mesh):
    return jax.shard_map(
        on_device,
        mesh=mesh,
        in_specs=(
            P("dp", None),
            P("dp", None),
            P("section", None),
            P("section", "dp", None),
            P("section", "dp", None),
            P(),
            P(),
            P(),
            P(),
            P("section", "dp", None),
            P("section", "dp", None),
            P("section", "dp", None),
        ),
        out_specs=(
            P("section", "dp", None),
            P("section", "dp", None),
            P("section", "dp", None),
            P("section", "dp", None),
        ),
        check_vma=False,
    )
```

```python
import jax
import jax.numpy as jnp
from jax import lax
from jax.experimental import pallas as pl
from jax.experimental.pallas import tpu as pltpu
from jax.sharding import PartitionSpec as P

ADAPTER_RANK = 16
MICRO = 4
LIMIT = 4
SECTIONS = 4
LAG = 2
CHUNK = 2048
RING = 4

ADAPTER_SCALE = 2.0
LEARN_RATE = 0.001
BETA_FIRST = 0.9
BETA_SECOND = 0.999
ADAM_EPS = 1e-08
FIRST_FIX = 1.0 - 0.9**50 * 0.9**50
SECOND_FIX = 1.0 - 0.999**50 * 0.999**50
NORM_EPS = 1e-05
F32 = jnp.float32
BF16 = jnp.bfloat16


def contract_trailing(left, right):
    return lax.dot_general(
        left, right, (((1,), (1,)), ((), ())), preferred_element_type=F32
    )


def contract_leading(left, right):
    return lax.dot_general(
        left, right, (((0,), (0,)), ((), ())), preferred_element_type=F32
    )


def plain_dot(left, right):
    return jnp.dot(left, right, preferred_element_type=F32)


def window(i):
    return pl.ds(pl.multiple_of(i * CHUNK, CHUNK), CHUNK)


VMEM_SPEC = pl.BlockSpec(memory_space=pltpu.VMEM)
SMEM_SPEC = pl.BlockSpec(memory_space=pltpu.SMEM)
FAR_SPEC = pl.BlockSpec(memory_space=pltpu.HBM)


def load_weight(pieces, chosen, lanes, section, base=None):
    features = lanes.stop - lanes.start
    sizes = [piece.shape[0] for piece in pieces]
    taken = [pieces[k] for k in chosen]
    rest = [] if base is None else [base]

    def kernel(*refs):
        target, sem = refs[-2:]
        for k, piece in zip(chosen, refs[: len(chosen)]):
            at = sum(sizes[:k])
            pltpu.make_async_copy(
                piece.at[:, lanes], target.at[at : at + sizes[k]], sem
            ).start()
        moved = target.at[0 : sum(sizes[k] for k in chosen)]
        pltpu.make_async_copy(moved, moved, sem).wait()

    return pl.pallas_call(
        kernel,
        in_specs=[FAR_SPEC] * len(taken) + [SMEM_SPEC] + [VMEM_SPEC] * len(rest),
        out_specs=VMEM_SPEC,
        out_shape=pltpu.VMEM((sum(sizes), features), BF16),
        scratch_shapes=[pltpu.SemaphoreType.DMA],
        input_output_aliases={len(taken) + 1: 0} if rest else {},
        compiler_params=pltpu.CompilerParams(vmem_limit_bytes=2**20),
        name="load_weight",
    )(*taken, section, *rest)


def chunk_loop(weight_ref, body):
    lax.fori_loop(0, weight_ref.shape[0] // CHUNK, lambda i, c: (body(window(i)), c)[1], 0)


def wide_product(rows_ref, weight_ref, total_ref):
    total_ref[...] = jnp.zeros_like(total_ref)

    def body(w):
        total_ref[...] += plain_dot(rows_ref[:, w], weight_ref[w, :])

    chunk_loop(weight_ref, body)


def call(kernel, name, outs, operands, scratch=(), alias=None, limit=LIMIT):
    return pl.pallas_call(
        kernel,
        in_specs=[SMEM_SPEC] + [VMEM_SPEC] * (len(operands) - 1),
        out_shape=tuple(jax.ShapeDtypeStruct(shape, dtype) for shape, dtype in outs),
        out_specs=(VMEM_SPEC,) * len(outs),
        scratch_shapes=list(scratch),
        input_output_aliases=alias or {},
        compiler_params=pltpu.CompilerParams(vmem_limit_bytes=limit * 2**20),
        name=name,
    )(*operands)


def ahead(section, step, value, output, down_t, up, token, received):
    choices = [x for x in (token, received) if x is not None]
    rows, width = choices[0].shape
    features = up.shape[1]
    lowest, highest = (step - MICRO) // LAG + 1, step // LAG

    def kernel(section_ref, value_ref, output_ref, down_ref, up_ref, *refs):
        sources = refs[: len(choices)]
        next_ref, u_ref, low_ref, scale_ref = refs[len(choices) : len(choices) + 4]
        here = section_ref[0]

        def run(h_ref):
            wide = h_ref[...].astype(F32)
            scale = lax.rsqrt(jnp.mean(wide * wide, axis=-1, keepdims=True) + NORM_EPS)
            low = contract_trailing(h_ref[...], down_ref[...])
            scale_ref[...] = scale
            low_ref[...] = low
            low = (scale * low).astype(BF16)
            wide_product(h_ref, value_ref, u_ref)
            v = (scale * u_ref[...] + ADAPTER_SCALE * plain_dot(low, up_ref[...])).astype(BF16)

            def body(w):
                next_ref[:, w] = (
                    h_ref[:, w].astype(F32) + contract_trailing(v, output_ref[w, :])
                ).astype(BF16)

            chunk_loop(output_ref, body)

        @pl.when((here >= lowest) & (here <= highest) & (here < SECTIONS - 1))
        def _():
            if len(choices) == 1:
                run(sources[0])
            else:
                picked = refs[-1]
                picked[...] = jnp.where(here == 0, sources[0][...], sources[1][...])
                run(picked)

    return call(
        kernel,
        "ahead",
        [((rows, width), BF16), ((rows, features), F32), ((rows, ADAPTER_RANK), F32), ((rows, 1), F32)],
        [section, value, output, down_t, up] + choices,
        scratch=[pltpu.VMEM((rows, width), BF16)] * (len(choices) - 1),
    )


def add_gradients(down_acc, up_acc, hidden, scale, low, gv, gl):
    scaled = (scale * gl.astype(F32)).astype(BF16)
    down_acc[...] += contract_leading(scaled, hidden)
    low_rows = (scale * low).astype(BF16)
    up_acc[...] += ADAPTER_SCALE * contract_leading(low_rows, gv)


def gradient_pair(acc_ref, up_ref):
    gv = acc_ref[...].astype(BF16)
    return gv, (ADAPTER_SCALE * contract_trailing(gv, up_ref[...])).astype(BF16)


def reverse(section, value, output, down_t, up, grad, saved, grads, base):
    rows, width = grad.shape
    features = up.shape[1]
    owners = sorted(saved)
    flat = [x for s in owners for x in saved[s]]

    def kernel(section_ref, value_ref, output_ref, down_ref, up_ref, grad_ref, *refs):
        sets = {s: refs[4 * k : 4 * k + 4] for k, s in enumerate(owners)}
        prev_ref, down_acc, up_acc, acc_ref = refs[-4:]
        here = section_ref[0]

        def pick(k):
            x = sets[owners[0]][k][...]
            return x if len(owners) == 1 else jnp.where(here == owners[0], x, sets[owners[1]][k][...])

        def pick_window(w):
            x = sets[owners[0]][0][:, w]
            return x if len(owners) == 1 else jnp.where(here == owners[0], x, sets[owners[1]][0][:, w])

        @pl.when((here >= owners[0]) & (here <= owners[-1]))
        def _():
            wide_product(grad_ref, output_ref, acc_ref)
            gv, gl = gradient_pair(acc_ref, up_ref)
            u, low, scale = pick(1), pick(2), pick(3)
            centred = (
                jnp.sum(gv.astype(F32) * u, axis=-1, keepdims=True)
                + jnp.sum(gl.astype(F32) * low, axis=-1, keepdims=True)
            ) / width
            coef = scale * scale * scale * centred

            def body(w):
                grad_norm = contract_trailing(gv, value_ref[w, :]) + plain_dot(gl, down_ref[:, w])
                prev_ref[:, w] = (
                    grad_ref[:, w].astype(F32)
                    + scale * grad_norm
                    - pick_window(w).astype(F32) * coef
                ).astype(BF16)

            chunk_loop(value_ref, body)
            add_gradients(down_acc, up_acc, pick(0), scale, low, gv, gl)

    operands = [section, value, output, down_t, up, grad] + flat + list(grads)
    first = len(operands) - 2
    alias = {first: 1, first + 1: 2}
    if base is not None:
        alias[len(operands)] = 0
        operands.append(base)
    return call(
        kernel,
        "reverse",
        [((rows, width), BF16), (grads[0].shape, F32), (grads[1].shape, F32)],
        operands,
        scratch=[pltpu.VMEM((rows, features), F32)],
        alias=alias,
    )


def reverse_first(section, output, up, grad, token, low, scale, grads):
    rows, features = grad.shape[0], up.shape[1]

    def kernel(section_ref, output_ref, up_ref, grad_ref, token_ref, low_ref, scale_ref, *refs):
        down_acc, up_acc, acc_ref = refs[2:]

        @pl.when(section_ref[0] == 0)
        def _():
            wide_product(grad_ref, output_ref, acc_ref)
            gv, gl = gradient_pair(acc_ref, up_ref)
            add_gradients(down_acc, up_acc, token_ref[...], scale_ref[...], low_ref[...], gv, gl)

    operands = [section, output, up, grad, token, low, scale] + list(grads)
    first = len(operands) - 2
    return call(
        kernel,
        "reverse_first",
        [(grads[0].shape, F32), (grads[1].shape, F32)],
        operands,
        scratch=[pltpu.VMEM((rows, features), F32)],
        alias={first: 0, first + 1: 1},
    )


def prepare(section, value, output, down_t, up, grad):
    rows, width = grad.shape
    features = up.shape[1]

    def kernel(section_ref, value_ref, output_ref, down_ref, up_ref, grad_ref, norm_ref, gv_ref, gl_ref, acc_ref):
        @pl.when(section_ref[0] == SECTIONS - 1)
        def _():
            wide_product(grad_ref, output_ref, acc_ref)
            gv, gl = gradient_pair(acc_ref, up_ref)
            gv_ref[...] = gv
            gl_ref[...] = gl

            def body(w):
                norm_ref[:, w] = contract_trailing(gv, value_ref[w, :]) + plain_dot(gl, down_ref[:, w])

            chunk_loop(value_ref, body)

    return call(
        kernel,
        "prepare",
        [((rows, width), F32), ((rows, features), BF16), ((rows, ADAPTER_RANK), BF16)],
        [section, value, output, down_t, up, grad],
        scratch=[pltpu.VMEM((rows, features), F32)],
    )


def join_last(section, down_t, hidden, grad_norm, gv, gl, grad, grads):
    rows, width = hidden.shape

    def kernel(section_ref, down_ref, h_ref, norm_ref, gv_ref, gl_ref, grad_ref, *refs):
        prev_ref, down_acc, up_acc = refs[2:]

        @pl.when(section_ref[0] == SECTIONS - 1)
        def _():
            wide = h_ref[...].astype(F32)
            norm = norm_ref[...]
            low = contract_trailing(h_ref[...], down_ref[...])
            scale = lax.rsqrt(jnp.mean(wide * wide, axis=-1, keepdims=True) + NORM_EPS)
            centred = jnp.mean(wide * norm, axis=-1, keepdims=True)
            prev_ref[...] = (
                grad_ref[...].astype(F32) + scale * norm - wide * (scale * scale * scale * centred)
            ).astype(BF16)
            add_gradients(down_acc, up_acc, h_ref[...], scale, low, gv_ref[...], gl_ref[...])

    operands = [section, down_t, hidden, grad_norm, gv, gl, grad] + list(grads)
    first = len(operands) - 2
    return call(
        kernel,
        "join_last",
        [((rows, width), BF16), (grads[0].shape, F32), (grads[1].shape, F32)],
        operands,
        alias={first: 1, first + 1: 2},
    )


def reorder_kernel(place_ref, tokens_ref, grads_ref, *refs):
    targets, sem = refs[: 2 * MICRO], refs[-1]
    rows = targets[0].shape[0]
    block = tokens_ref.shape[1] // place_ref.shape[0]

    def copy_of(slot, k):
        source = (tokens_ref, grads_ref)[k // MICRO]
        m = k % MICRO
        origin = pl.multiple_of(place_ref[slot] * block, block)
        goal = pl.multiple_of(slot * block, block)
        return pltpu.make_async_copy(
            source.at[m * rows : (m + 1) * rows, pl.ds(origin, block)],
            targets[k].at[:, pl.ds(goal, block)],
            sem.at[k],
        )

    def begin(slot, carry):
        for k in range(2 * MICRO):
            copy_of(slot, k).start()
        return carry

    lax.fori_loop(0, place_ref.shape[0], begin, 0)
    for k in range(2 * MICRO):
        pltpu.make_async_copy(targets[k], targets[k], sem.at[k]).wait()


def reorder(place, tokens, grads):
    rows = tokens.shape[0] // MICRO
    return pl.pallas_call(
        reorder_kernel,
        in_specs=[pl.BlockSpec(memory_space=pltpu.SMEM), FAR_SPEC, FAR_SPEC],
        out_specs=(FAR_SPEC,) * (2 * MICRO),
        out_shape=(jax.ShapeDtypeStruct((rows, tokens.shape[1]), BF16),) * (2 * MICRO),
        scratch_shapes=[pltpu.SemaphoreType.DMA((2 * MICRO,))],
        compiler_params=pltpu.CompilerParams(vmem_limit_bytes=2**20),
        name="reorder",
    )(place, tokens, grads)


def torus_shift(first, by):
    pairs = []
    for y in range(RING):
        for z in range(RING):
            for core in range(2):
                along_y = (core == 0) == first
                ty, tz = ((y + by) % RING, z) if along_y else (y, (z + by) % RING)
                pairs.append(((y * RING + z) * 2 + core, (ty * RING + tz) * 2 + core))
    return pairs


def ring_pieces(head, tail, first, between=lambda x: x):
    up_pairs, down_pairs = torus_shift(first, 1), torus_shift(first, -1)
    before_head = lax.ppermute(head, "dp", up_pairs)
    after_tail = lax.ppermute(tail, "dp", down_pairs)
    before_tail = lax.ppermute(tail, "dp", up_pairs)
    after_head = lax.ppermute(head, "dp", down_pairs)
    before_head, after_tail = between((before_head, after_tail))
    far_head = lax.ppermute(before_head, "dp", up_pairs)
    far_tail = lax.ppermute(after_tail, "dp", down_pairs)
    return [head, tail, before_head, before_tail, after_head, after_tail, far_head, far_tail]


def near_groups(block):
    half = block.shape[0] // 2
    near = ring_pieces(block[:half], block[half:], True)
    return jnp.concatenate(near[:4], axis=0), jnp.concatenate(near[4:], axis=0)


def far_pieces(group_head, group_tail, between):
    mine = ring_pieces(group_head, group_tail, False, between)
    swap = [(i, i ^ 1) for i in range(2 * RING * RING)]
    pieces = mine + [lax.ppermute(piece, "dp", swap) for piece in mine]
    return [pltpu.with_memory_space_constraint(piece, pltpu.HBM) for piece in pieces]


def slot_places(owner_index):
    offsets = jnp.array([0, -1, 1, 2], jnp.int32)
    core = owner_index % 2
    chip = owner_index // 2
    y, z = chip // RING, chip % RING
    outer = jnp.repeat(offsets, RING)
    inner = jnp.tile(offsets, RING)
    by_y = ((y + inner) % RING * RING + (z + outer) % RING) * 2
    by_z = ((y + outer) % RING * RING + (z + inner) % RING) * 2 + 1
    return jnp.where(core == 0, jnp.concatenate([by_y, by_z]), jnp.concatenate([by_z, by_y]))


def adam_update(params_old, first_old, second_old, slot_grad, live):
    first_step = BETA_FIRST * first_old + (1.0 - BETA_FIRST) * slot_grad
    second_step = BETA_SECOND * second_old + (1.0 - BETA_SECOND) * slot_grad * slot_grad
    step_size = first_step / FIRST_FIX / (jnp.sqrt(second_step / SECOND_FIX) + ADAM_EPS)
    params_step = (params_old.astype(jnp.float32) - LEARN_RATE * step_size).astype(jnp.bfloat16)
    return (
        jnp.where(live, params_step, params_old),
        jnp.where(live, first_step, first_old),
        jnp.where(live, second_step, second_old),
    )


def on_device(
    tokens,
    cotangent,
    gains,
    value_projection_weight,
    output_projection_weight,
    block_adapter_ids,
    job_adapter,
    job_slab,
    token_counts,
    slot_adapter_params,
    first_moment,
    second_moment,
):
    section_index = lax.axis_index("section")
    owner_index = lax.axis_index("dp")
    section_total = lax.axis_size("section")
    owner_total = lax.axis_size("dp")
    tok_dev, hidden_width = tokens.shape
    value_feature_width = value_projection_weight.shape[2]
    panel_width = slot_adapter_params.shape[2]
    slab_count = owner_total // 2
    block_total = block_adapter_ids.shape[0]
    local_blocks = block_total // owner_total
    block_rows = tok_dev // local_blocks
    adapter_total = token_counts.shape[0]
    divide_position = hidden_width * ADAPTER_RANK
    gain_row = gains[0]
    shard_rows = value_projection_weight.shape[1]
    my_gain = lax.dynamic_slice_in_dim(gain_row, owner_index * shard_rows, shard_rows)
    scaled_value = (value_projection_weight[0].astype(F32) * my_gain[:, None]).astype(BF16)
    my_jobs = lax.dynamic_index_in_dim(job_adapter, owner_index, 0, keepdims=False)
    my_blocks = lax.dynamic_slice_in_dim(
        block_adapter_ids, owner_index * local_blocks, local_blocks
    )
    slab_ids = jnp.arange(slab_count, dtype=jnp.int32)
    matching = (job_adapter[None, None] == my_blocks[:, None, None, None]) & (
        job_slab[None, None] == slab_ids[None, :, None, None]
    )
    owner_ids = jnp.arange(owner_total, dtype=jnp.int32)
    source_owner = jnp.sum(jnp.where(matching, owner_ids[None, None, :, None], 0), axis=(2, 3))
    own_select = (block_adapter_ids[:, None] == my_jobs[None, :]) & (my_jobs[None, :] >= 0)
    slot_rows = jnp.arange(local_blocks, dtype=jnp.int32)[:, None]

    def hand_out(owned):
        picked = jnp.dot(own_select.astype(jnp.bfloat16), owned, preferred_element_type=jnp.float32)
        return picked.astype(jnp.bfloat16).reshape(owner_total, local_blocks, panel_width)

    def assemble(arrived):
        gathered_slabs = arrived[source_owner, slot_rows]
        return gathered_slabs.reshape(local_blocks, slab_count * panel_width)

    arrived_panels = lax.all_to_all(
        hand_out(slot_adapter_params[0]), "dp", split_axis=0, concat_axis=0, tiled=True
    )
    blocks_of = lambda flat: flat.reshape(owner_total, -1)

    def set_up(inputs):
        panels, tokens, cotangent, gain_row, places = inputs
        reordered = reorder(places, tokens, cotangent)
        token_micro, cot_micro = list(reordered[:MICRO]), list(reordered[MICRO:])
        gathered = assemble(panels)
        gain_slots = blocks_of(gain_row)[places].reshape(-1)
        down_t = (
            blocks_of(gathered[0, :divide_position])[places]
            .reshape(hidden_width, ADAPTER_RANK)
            .T.astype(F32)
            * gain_slots[None, :]
        ).astype(BF16)
        up = gathered[0, divide_position:].reshape(ADAPTER_RANK, value_feature_width)
        return token_micro, cot_micro, gain_slots, down_t, up

    inputs = (arrived_panels, tokens, cotangent, gain_row, slot_places(owner_index))
    block = jnp.concatenate([scaled_value, output_projection_weight[0]], axis=1)
    group_head, group_tail = near_groups(block)
    group_head, group_tail, inputs = lax.optimization_barrier((group_head, group_tail, inputs))
    places = inputs[-1]
    ready = set_up(inputs)
    kept = []

    def between(arrived):
        arrived, early = lax.optimization_barrier((arrived, ready))
        kept.append(early)
        return arrived

    pieces = far_pieces(group_head, group_tail, between)
    token_micro, cot_micro, gain_slots, down_t, up = kept[0]
    prepared = []
    last = section_total - 1
    ahead_pairs = [(i, i + 1) for i in range(last)]
    back_pairs = [(i + 1, i) for i in range(last)]
    section = jnp.full((1,), section_index, jnp.int32)
    grads = (
        jnp.zeros((ADAPTER_RANK, hidden_width), F32),
        jnp.zeros((ADAPTER_RANK, value_feature_width), F32),
    )
    section, grads, token_micro = lax.optimization_barrier((section, grads, token_micro))
    early, late = range(len(pieces) - 2), range(len(pieces) - 2, len(pieces))
    value_lanes = slice(0, value_feature_width)
    output_lanes = slice(value_feature_width, 2 * value_feature_width)
    value = load_weight(pieces, early, value_lanes, section)
    output = load_weight(pieces, early, output_lanes, section)
    value = load_weight(pieces, late, value_lanes, section, value)
    output = load_weight(pieces, late, output_lanes, section, output)

    entering, ahead_state, ahead_sent, back_sent = {}, {}, {}, {}
    for step in range(2 * last * LAG + MICRO):
        if step - LAG in ahead_sent:
            entering[step] = ahead_sent[step - LAG]
        if step < (last - 1) * LAG + MICRO:
            token = token_micro[step] if step < MICRO else None
            result = ahead(section, step, value, output, down_t, up, token, entering.get(step))
            ahead_state[step] = result[1:]
            ahead_sent[step] = lax.ppermute(result[0], "section", ahead_pairs)
        if step < MICRO:
            done = prepare(section, value, output, down_t, up, cot_micro[step])
            section, *done = lax.optimization_barrier((section,) + tuple(done))
            prepared.append(done)
        incoming = back_sent.get(step - LAG)
        m = step - LAG * last
        outgoing_rows = None
        if 0 <= m < MICRO:
            norm, gv, gl = prepared[m]
            outgoing_rows, *grads = join_last(
                section, down_t, entering[step], norm, gv, gl, cot_micro[m], grads
            )
        saved = {}
        for s in range(1, last):
            m = step - LAG * (2 * last - s)
            if 0 <= m < MICRO:
                saved[s] = (entering[LAG * s + m],) + tuple(ahead_state[LAG * s + m])
        if saved:
            back, *grads = reverse(section, value, output, down_t, up, incoming, saved, grads, outgoing_rows)
            outgoing_rows = back
        if outgoing_rows is not None:
            back_sent[step] = lax.ppermute(outgoing_rows, "section", back_pairs)
        m = step - LAG * 2 * last
        if 0 <= m < MICRO:
            _, low, scale = ahead_state[m]
            grads = reverse_first(
                section, output, up, incoming, token_micro[m], low, scale, grads
            )

    natural = jnp.sum(
        jnp.where(places[None, :] == owner_ids[:, None], owner_ids[None, :], 0), axis=1
    )
    down_grad = (grads[0] * gain_slots[None, :]).astype(BF16).T
    block_grads = jnp.concatenate(
        [blocks_of(down_grad)[natural].reshape(-1), grads[1].astype(BF16).reshape(-1)]
    )
    outgoing = (
        jnp.zeros((owner_total, local_blocks, panel_width), BF16)
        .at[source_owner, slot_rows]
        .set(block_grads.reshape(local_blocks, slab_count, panel_width))
    )
    arrived = lax.all_to_all(outgoing, "dp", split_axis=0, concat_axis=0, tiled=True)
    summed = jnp.dot(
        own_select.astype(BF16).T,
        arrived.reshape(block_total, panel_width),
        preferred_element_type=F32,
    )
    live = my_jobs >= 0
    adapter_ids = jnp.arange(adapter_total, dtype=jnp.int32)
    slot_counts = jnp.sum(
        jnp.where(adapter_ids[None, :] == my_jobs[:, None], token_counts[None, :], 0), axis=1
    )
    slot_counts = jnp.where(live, slot_counts, 1)
    slot_grad = summed / slot_counts.astype(jnp.float32)[:, None]
    params_new, first_new, second_new = adam_update(
        slot_adapter_params[0], first_moment[0], second_moment[0], slot_grad, live[:, None]
    )
    returned = assemble(
        lax.all_to_all(hand_out(params_new), "dp", split_axis=0, concat_axis=0, tiled=True)
    )
    return (params_new[None], first_new[None], second_new[None], returned[None])


def solution(mesh):
    return jax.shard_map(
        on_device,
        mesh=mesh,
        in_specs=(
            P("dp", None),
            P("dp", None),
            P("section", None),
            P("section", "dp", None),
            P("section", "dp", None),
            P(),
            P(),
            P(),
            P(),
            P("section", "dp", None),
            P("section", "dp", None),
            P("section", "dp", None),
        ),
        out_specs=(
            P("section", "dp", None),
            P("section", "dp", None),
            P("section", "dp", None),
            P("section", "dp", None),
        ),
        check_vma=False,
    )
```
